128 devices in a mesh: seq: 32 (over x, z, core), head: 4 (over y).
Axes of the slice: x: 4, y: 4, z: 4, core: 2. Of those that a mesh axis runs over, the one named last changes fastest.
Arguments:
- tokens: bfloat16 [32768, 2048], P('seq', 'head'), may hold values from -64 to 64
- project_weights: bfloat16 [2048, 3, 2048], P(None, None, 'head'), may hold values from -0.125 to 0.125
- output_weights: bfloat16 [2048, 2048], P('head'), may hold values from -0.125 to 0.125
- cluster_ids: int32 [16, 32768, 1], P('head', 'seq'), may hold values from 0 to 255; in each aligned block of 1024 rows (0 to 1023, 1024 to 2047, ..., all dimensions but the last counted through in order) at most 8 rows name the same one
Outputs:
- mixed: bfloat16 [32768, 2048], P('seq', 'head')
- key_sums: float32 [16, 256, 128], P('head', 'seq')
The draws below stay inside these ranges and needn't reach their ends.
Inputs may be any that keep to these rules, and one draw needn't show every extreme that they name: `cluster_ids`: in each head, the 1024 rows of one index of seq name no cluster more than 8 times.
All inputs are finite; a program needn't handle non-finite values.
Results may differ from the reference program's by a relative error of at most 0.012.
The reference program's roundings to bfloat16 on the way (of `weights`, `attended` and `unit_keys`) count: a program that leaves them out, or rounds other values in their place, can miss the bound.
Values may be sent and summed in bfloat16 or wider, within the bound.
No kernel may reach another device: no remote copies, remote signals or barrier semaphores. Data moves between devices by JAX's collectives and lax.ppermute only.
A program may use at most 128 MiB of HBM per device.

```python
import math
import jax
import jax.numpy as jnp
import numpy as np
from jax import lax

D = 2048
HEADS = 16
HEAD_DIM = 128
CLUST_DEV = 8
TOK_DEV = 1024
CLUSTERS = 256
TOKENS = 32768
SLOT = 8
BUCKET = 256
N_SEQ = 32


def draw_tokens(key, part):
    normal_key = jax.random.fold_in(key, 11)
    base = jax.random.truncated_normal(normal_key, -4.0, 4.0, (TOKENS, D), jnp.float32)
    return base.astype(jnp.bfloat16)


def block_levels(stream_key, dims, split, smallest, largest):
    def one(axis_at, shards_of):
        steps = jax.random.uniform(jax.random.fold_in(jax.random.fold_in(stream_key, 6), axis_at), (shards_of,), jnp.float32, smallest / len(split), largest / len(split))
        return jnp.repeat(jnp.exp(steps), dims[axis_at] // shards_of).reshape((-1,) + (1,) * (len(dims) - axis_at - 1))

    loudness = one(*split[0])
    for cut in split[1:]:
        loudness = loudness * one(*cut)
    return loudness


def assign_block(stream_key, own, number, rows, count, top, bound, skew):
    order = jax.random.permutation(stream_key, count)
    packed, ordinary = load_shares(count, rows * top, bound, skew, True), load_shares(count, rows * top, bound, skew, False)
    places = jnp.arange(count)

    def named(lengths, rotation):
        used = int((lengths > 0).sum())
        fixed = max(1, used // 4)
        shifted = fixed + (places - fixed + rotation * (used - fixed)) % max(1, count - fixed)
        return jnp.zeros((count,), jnp.int32).at[order[jnp.where(places < fixed, places, shifted)]].set(jnp.asarray(lengths, jnp.int32))

    lengths = jnp.where(number % 4 == 0, named(packed, number // 4), named(ordinary, number - number // 4 - 1))
    mixed = jax.random.permutation(jax.random.fold_in(own, 3), count)
    donor, receiver = mixed[0:count // 2 * 2:2], mixed[1:count // 2 * 2:2]
    slack = jnp.minimum(lengths[donor] - 1, bound - lengths[receiver]) // 2
    slack = jnp.where((donor == order[0]) | (receiver == order[0]) | (lengths[receiver] == 0), 0, jnp.maximum(slack, 0))
    shifted = jax.random.randint(jax.random.fold_in(own, 4), (count // 2,), 0, 1 << 20) % (slack + 1)
    lengths = lengths.at[donor].add(-shifted).at[receiver].add(shifted)
    items = jnp.searchsorted(jnp.cumsum(lengths), jnp.arange(rows * top), side="right").astype(jnp.int32)
    listing = items.reshape(top, rows).T
    listing = listing[jax.random.permutation(jax.random.fold_in(own, 1), rows)]
    rotation = jax.random.randint(jax.random.fold_in(own, 2), (rows, 1), 0, top)
    return jnp.take_along_axis(listing, (jnp.arange(top)[None, :] + rotation) % top, axis=1)


def load_shares(amount, total, limit, skew, full):
    loads = [(1 << 20) // math.isqrt(rank ** skew) + 1 for rank in range(1, amount + 1)]
    largest = limit if full else min(limit, max(-(-total // amount), total * loads[0] // sum(loads)))
    least = 1 if total - largest >= amount - 1 else 0
    given, spare = [largest] + [least] * (amount - 1), total - largest - least * (amount - 1)
    while spare > 0:
        free = [i for i in range(1, amount) if given[i] < largest] or [i for i in range(1, amount) if given[i] < limit]
        whole, left = sum([loads[i] for i in free]), spare
        for i in free:
            more = min(limit - given[i], max(1, left * loads[i] // whole), spare)
            given[i] = given[i] + more
            spare = spare - more
    return np.array(given)


def normal_values(key, shape, scale, most, split=(), kind=jnp.bfloat16):
    factor_of = block_levels(key, shape, split, -0.22, 0.18) if split else 1.0
    entries = jax.random.normal(key, shape, jnp.float32) * scale * factor_of
    return jnp.minimum(jnp.maximum(entries, -most), most).astype(kind)


def setup_inputs(seed: int = 0) -> dict:
    seeds = jax.random.split(jax.random.key(seed), 5)
    tokens = draw_tokens(jax.random.fold_in(seeds[4], 71), 0)
    project_weights = normal_values(seeds[1], (D, 3, D), D ** -0.5, 0.125, ((2, 4),))
    output_weights = normal_values(seeds[2], (D, D), D ** -0.5, 0.125, ((0, 4),))
    cluster_ids_keys = jax.random.split(jax.random.fold_in(seeds[3], 1), HEADS * TOKENS // TOK_DEV)
    cluster_ids_turns = jax.random.permutation(jax.random.fold_in(seeds[3], 3), HEADS * TOKENS // TOK_DEV)
    cluster_ids = jax.vmap(lambda own, number: assign_block(jax.random.fold_in(seeds[3], 2), own, number, TOK_DEV, CLUSTERS, 1, SLOT, 1))(cluster_ids_keys, cluster_ids_turns).reshape((HEADS, TOKENS, 1))
    return {"tokens": tokens, "project_weights": project_weights, "output_weights": output_weights, "cluster_ids": cluster_ids}


def unit_rows(key_array):
    key_float = key_array.astype(jnp.float32)
    scaled = key_float * lax.rsqrt(lax.optimization_barrier(jnp.mean(key_float * key_float, axis=-1, keepdims=True)) + 1e-06)
    return (scaled / math.sqrt(key_array.shape[-1])).astype(jnp.bfloat16)

def attend_group(operands):
    query_group, key_group, value_group, live_group = operands
    score_scale = 1.0 / math.sqrt(query_group.shape[-1])
    scores = jnp.einsum('gqd,gkd->gqk', query_group.astype(jnp.float32), key_group.astype(jnp.float32)) * score_scale
    bucket_iota = jnp.arange(scores.shape[-1], dtype=jnp.int32)
    causal = bucket_iota[None, :] <= bucket_iota[:, None]
    allowed = causal[None] & live_group[:, None, :]
    scores = jnp.where(allowed, scores, -1e+30)
    row_max = lax.optimization_barrier(jnp.max(scores, axis=-1, keepdims=True))
    exponentials = jnp.exp(scores - row_max)
    weights = (exponentials / lax.optimization_barrier(jnp.sum(exponentials, axis=-1, keepdims=True))).astype(jnp.bfloat16)
    return jnp.einsum('gqk,gkd->gqd', weights.astype(jnp.float32), value_group.astype(jnp.float32)).astype(jnp.bfloat16)

def one_head(operands):
    queries, key_rows, values, assigned = operands
    sorted_order = jnp.argsort(assigned, stable=True).astype(jnp.int32)
    inverse = jnp.argsort(sorted_order).astype(jnp.int32)
    counts = jax.ops.segment_sum(jnp.ones_like(assigned), assigned, num_segments=CLUSTERS).astype(jnp.int32)
    starts = (jnp.cumsum(counts) - counts).astype(jnp.int32)
    bucket_iota = jnp.arange(BUCKET, dtype=jnp.int32)
    positions = jnp.minimum(starts[:, None] + bucket_iota[None, :], TOKENS - 1)
    members = sorted_order[positions]
    live_slots = bucket_iota[None, :] < counts[:, None]
    grouped = (queries[members].reshape(CLUST_DEV, N_SEQ, BUCKET, HEAD_DIM), key_rows[members].reshape(CLUST_DEV, N_SEQ, BUCKET, HEAD_DIM), values[members].reshape(CLUST_DEV, N_SEQ, BUCKET, HEAD_DIM), live_slots.reshape(CLUST_DEV, N_SEQ, BUCKET))
    bucket_out = lax.map(attend_group, grouped).reshape(CLUSTERS, BUCKET, HEAD_DIM)
    slot_rank = (inverse - starts[assigned]).astype(jnp.int32)
    attended = bucket_out[assigned, slot_rank]
    unit_keys = unit_rows(key_rows)
    key_total = jax.ops.segment_sum(unit_keys.astype(jnp.float32), assigned, num_segments=CLUSTERS)
    return (attended, key_total)

def reference(tokens, project_weights, output_weights, cluster_ids):
    queries = jnp.dot(tokens, project_weights[:, 0, :], preferred_element_type=jnp.float32).astype(jnp.bfloat16)
    key_rows = jnp.dot(tokens, project_weights[:, 1, :], preferred_element_type=jnp.float32).astype(jnp.bfloat16)
    values = jnp.dot(tokens, project_weights[:, 2, :], preferred_element_type=jnp.float32).astype(jnp.bfloat16)
    per_head = (queries.reshape(TOKENS, HEADS, HEAD_DIM).transpose(1, 0, 2), key_rows.reshape(TOKENS, HEADS, HEAD_DIM).transpose(1, 0, 2), values.reshape(TOKENS, HEADS, HEAD_DIM).transpose(1, 0, 2), cluster_ids[:, :, 0].astype(jnp.int32))
    attended, key_sums = lax.map(one_head, per_head)
    attended = attended.transpose(1, 0, 2).reshape(TOKENS, D)
    mixed = jnp.dot(attended, output_weights, preferred_element_type=jnp.float32).astype(jnp.bfloat16)
    return (mixed, key_sums)
```

```python
import functools
import math

import jax
import jax.numpy as jnp
from jax import lax
from jax.experimental import pallas as pl
from jax.experimental.pallas import tpu as pltpu
from jax.sharding import Mesh
from jax.sharding import PartitionSpec as P

HEAD_DIM = 128
CLUST_DEV = 8
SLOT = 8
SEQ = ("seq_0", "seq_1", "seq_2")
F32 = jnp.float32
BF16 = jnp.bfloat16


def shifted(array, by):
    count = lax.axis_size("head")
    return lax.ppermute(array, "head", [(i, (i + by) % count) for i in range(count)])


def params(**more):
    return pltpu.CompilerParams(vmem_limit_bytes=56 * 1024 * 1024, **more)


def first_blocks_kernel(where, own, left, right, w_own, w_left, w_right, out):
    total = jnp.dot(own[...], w_own[0], preferred_element_type=F32)
    total += jnp.dot(left[...], w_left[0], preferred_element_type=F32)
    total += jnp.dot(right[...], w_right[0], preferred_element_type=F32)
    out[0] = total


def first_blocks(where, own, left, right, weights):
    kinds, _, width = weights.shape
    rows, depth = own.shape
    whole = pl.BlockSpec((rows, depth), lambda j, w: (0, 0))
    return pl.pallas_call(
        first_blocks_kernel,
        out_shape=jax.ShapeDtypeStruct((kinds, rows, width), F32),
        grid_spec=pltpu.PrefetchScalarGridSpec(
            num_scalar_prefetch=1,
            grid=(kinds,),
            in_specs=[whole, whole, whole]
            + [pl.BlockSpec((1, depth, width), functools.partial(lambda b, j, w: (j, w[b], 0), b)) for b in range(3)],
            out_specs=pl.BlockSpec((1, rows, width), lambda j, w: (j, 0, 0)),
        ),
        compiler_params=params(),
        name="first_blocks",
    )(where, own, left, right, weights, weights, weights)


def pack_kernel(where, part, far_top, far_bottom, w_far, slot_of, out, projected):
    head = pl.program_id(0)
    kinds, rows, width = part.shape
    half = rows // 2
    heads = width // HEAD_DIM

    @pl.when(head == 0)
    def _():
        for kind in range(kinds):
            top = part[kind, :half] + jnp.dot(far_top[...], w_far[kind], preferred_element_type=F32)
            bottom = part[kind, half:] + jnp.dot(far_bottom[...], w_far[kind], preferred_element_type=F32)
            for h in range(heads):
                cols = slice(h * HEAD_DIM, (h + 1) * HEAD_DIM)
                to = slice(kind * HEAD_DIM, (kind + 1) * HEAD_DIM)
                projected[h, :half, to] = top[:, cols].astype(BF16)
                projected[h, half:, to] = bottom[:, cols].astype(BF16)

    rows_in = projected[head]
    slot_row = slot_of[0]
    devices, _, per_device, _ = out.shape
    step = 4
    chunk = step * per_device

    def body(i, carry):
        iota = lax.broadcasted_iota(jnp.int32, (chunk, rows), 0) + i * chunk
        onehot = jnp.where(iota == slot_row, 1.0, 0.0).astype(BF16)
        packed = jnp.dot(onehot, rows_in, preferred_element_type=F32).astype(BF16)
        out[pl.ds(i * step, step), 0] = packed.reshape(step, per_device, packed.shape[-1])
        return carry

    lax.fori_loop(0, devices // step, body, 0, unroll=2)


def pack(where, part, far_top, far_bottom, weights, slot_index, devices):
    kinds, rows, width = part.shape
    heads = width // HEAD_DIM
    depth = far_top.shape[1]
    lanes = kinds * HEAD_DIM
    per_device = CLUST_DEV * SLOT
    return pl.pallas_call(
        pack_kernel,
        out_shape=jax.ShapeDtypeStruct((devices, heads, per_device, lanes), BF16),
        grid_spec=pltpu.PrefetchScalarGridSpec(
            num_scalar_prefetch=1,
            grid=(heads,),
            in_specs=[
                pl.BlockSpec((kinds, rows, width), lambda h, w: (0, 0, 0)),
                pl.BlockSpec((rows // 2, depth), lambda h, w: (0, 0)),
                pl.BlockSpec((rows // 2, depth), lambda h, w: (0, 0)),
                pl.BlockSpec((kinds, depth, width), lambda h, w: (0, w[3], 0)),
                pl.BlockSpec((1, 1, rows), lambda h, w: (h, 0, 0)),
            ],
            out_specs=pl.BlockSpec((devices, 1, per_device, lanes), lambda h, w: (0, h, 0, 0)),
            scratch_shapes=[pltpu.VMEM((heads, rows, lanes), BF16)],
        ),
        compiler_params=params(),
        name="pack",
    )(where, part, far_top, far_bottom, weights, slot_index[:, None, :])


def attend_kernel(received, bias, out):
    devices, heads, _, slot, _ = received.shape
    bucket = devices * slot
    scale = 1.0 / math.sqrt(HEAD_DIM)
    rows = lax.broadcasted_iota(jnp.int32, (bucket, bucket), 0)
    cols = lax.broadcasted_iota(jnp.int32, (bucket, bucket), 1)
    causal = cols <= rows
    for h in range(heads):
        both = received[:, h, 0].reshape(bucket, 3 * HEAD_DIM)
        query, key, value = (both[:, i * HEAD_DIM : (i + 1) * HEAD_DIM] for i in range(3))
        scores = lax.dot_general(query, key, (((1,), (1,)), ((), ())), preferred_element_type=F32) * scale
        scores = jnp.where(causal & (bias[0, h : h + 1] > 0), scores, -1e30)
        row_max = jnp.max(scores, axis=-1, keepdims=True)
        exponentials = jnp.exp(scores - row_max)
        weights = (exponentials / jnp.sum(exponentials, axis=-1, keepdims=True)).astype(BF16)
        result = jnp.dot(weights, value, preferred_element_type=F32).astype(BF16)
        out[:, h, 0] = result.reshape(devices, slot, HEAD_DIM)


def attend(received, live):
    devices, heads, clusters, slot, lanes = received.shape
    bucket = devices * slot
    return pl.pallas_call(
        attend_kernel,
        out_shape=jax.ShapeDtypeStruct((devices, heads, clusters, slot, HEAD_DIM), BF16),
        grid=(clusters,),
        in_specs=[
            pl.BlockSpec((devices, heads, 1, slot, lanes), lambda c: (0, 0, c, 0, 0)),
            pl.BlockSpec((1, heads, bucket), lambda c: (c, 0, 0)),
        ],
        out_specs=pl.BlockSpec((devices, heads, 1, slot, HEAD_DIM), lambda c: (0, 0, c, 0, 0)),
        compiler_params=params(),
        name="attend",
    )(received, live)


def key_sums_kernel(keys, out):
    devices, heads, _, slot, width = keys.shape
    for h in range(heads):
        key = keys[:, h, 0].astype(F32)
        scaled = key * lax.rsqrt(jnp.mean(key * key, axis=-1, keepdims=True) + 1e-06)
        unit = (scaled / math.sqrt(width)).astype(BF16).astype(F32)
        out[0, h : h + 1] = jnp.sum(jnp.sum(unit, axis=0), axis=0, keepdims=True)


def key_sums(received):
    devices, heads, clusters, slot, _ = received.shape
    return pl.pallas_call(
        key_sums_kernel,
        out_shape=jax.ShapeDtypeStruct((clusters, heads, HEAD_DIM), F32),
        grid=(clusters,),
        in_specs=[pl.BlockSpec((devices, heads, 1, slot, HEAD_DIM), lambda c: (0, 0, c, 0, 1))],
        out_specs=pl.BlockSpec((1, heads, HEAD_DIM), lambda c: (c, 0, 0)),
        compiler_params=params(),
        name="key_sums",
    )(received)


def unpack_kernel(returned, slot_of, out):
    devices, _, per_device, width = returned.shape
    slots = devices * per_device
    rows = out.shape[0]
    source = returned[:, 0].reshape(slots, width)
    chunk = 256

    def body(i, carry):
        at = pl.ds(pl.multiple_of(i * chunk, chunk), chunk)
        iota = lax.broadcasted_iota(jnp.int32, (chunk, slots), 1)
        onehot = jnp.where(iota == slot_of[0, at], 1.0, 0.0).astype(BF16)
        out[at] = jnp.dot(onehot, source, preferred_element_type=F32).astype(BF16)
        return carry

    lax.fori_loop(0, rows // chunk, body, 0, unroll=2)


def unpack(returned, slot_index):
    devices, heads, per_device, width = returned.shape
    rows = slot_index.shape[1]
    return pl.pallas_call(
        unpack_kernel,
        out_shape=jax.ShapeDtypeStruct((rows, heads * width), BF16),
        grid=(heads,),
        in_specs=[
            pl.BlockSpec((devices, 1, per_device, width), lambda h: (0, h, 0, 0)),
            pl.BlockSpec((1, rows, 1), lambda h: (h, 0, 0)),
        ],
        out_specs=pl.BlockSpec((rows, width), lambda h: (0, h)),
        compiler_params=params(),
        name="unpack",
    )(returned, slot_index[:, :, None])


def ring(block):
    half = block.shape[0] // 2
    left = shifted(block, 1)
    right = shifted(block, -1)
    return left, right, shifted(left[:half], 1), shifted(right[half:], -1)


def local(tokens, project_weights, output_weights, cluster_ids):
    seq_count = lax.axis_size(SEQ)
    groups = lax.axis_size("head")
    here = lax.axis_index("head")
    width = output_weights.shape[0]
    heads = width // HEAD_DIM
    rows = tokens.shape[0]
    clusters = CLUST_DEV * seq_count

    assigned = cluster_ids[:, :, 0]
    matches = assigned[:, :, None] == jnp.arange(clusters, dtype=jnp.int32)
    counts = jnp.sum(matches.astype(jnp.int32), axis=1)
    row_iota = jnp.arange(rows, dtype=jnp.int32)
    earlier = (row_iota[None, :] < row_iota[:, None]).astype(BF16)
    before = jnp.einsum("ts,hsc->htc", earlier, matches.astype(BF16), preferred_element_type=F32)
    slot_rank = jnp.sum(jnp.where(matches, before, 0.0), axis=2).astype(jnp.int32)
    slot_index = assigned * SLOT + slot_rank

    by_owner = counts.T.reshape(seq_count, CLUST_DEV, heads)
    filled = lax.all_to_all(by_owner, SEQ, 0, 0, tiled=True)
    live = (filled.transpose(1, 2, 0)[..., None] > jnp.arange(SLOT, dtype=jnp.int32)).astype(F32)
    live = live.reshape(CLUST_DEV, heads, seq_count * SLOT)

    weights = project_weights.transpose(1, 0, 2)
    where = jnp.stack([here, (here - 1) % groups, (here + 1) % groups, (here + 2) % groups]).astype(jnp.int32)
    left, right, far_top, far_bottom = ring(tokens)
    part = first_blocks(where, tokens, left, right, weights)
    packed = pack(where, part, far_top, far_bottom, weights, slot_index, seq_count)

    received = lax.all_to_all(packed, SEQ, 0, 0, tiled=True)

    out_weights, _ = lax.optimization_barrier((output_weights, far_top))
    out_blocks = []
    for by in range(groups):
        block = lax.dynamic_slice(out_weights, (0, (here + by) % groups * width), (width, width))
        out_blocks.append(shifted(block, by) if by else block)

    received = received.reshape(seq_count, heads, CLUST_DEV, SLOT, 3 * HEAD_DIM)
    bucket_out = attend(received, live)
    owned = key_sums(received)
    returned = lax.all_to_all(bucket_out.reshape(seq_count, heads, CLUST_DEV * SLOT, HEAD_DIM), SEQ, 0, 0, tiled=True)
    attended = unpack(returned, slot_index)
    left, right, far_top, far_bottom = ring(attended)

    def times(block, by):
        return jnp.dot(block, out_blocks[by], preferred_element_type=F32)

    near = times(attended, 0) + times(left, 1) + times(right, 3)
    mixed = (near + times(jnp.concatenate([far_top, far_bottom]), 2)).astype(BF16)
    return (mixed, owned.transpose(1, 0, 2))


def solution(mesh):
    split = Mesh(
        mesh.devices.reshape(4, 4, 2, mesh.shape["head"]), ("seq_0", "seq_1", "seq_2", "head")
    )
    in_specs = (P(SEQ, "head"), P(None, None, "head"), P("head", None), P("head", SEQ, None))
    out_specs = (P(SEQ, "head"), P("head", SEQ, None))
    return jax.shard_map(local, mesh=split, in_specs=in_specs, out_specs=out_specs, check_vma=False)
```

```python
import functools
import math

import jax
import jax.numpy as jnp
from jax import lax
from jax.experimental import pallas as pl
from jax.experimental.pallas import tpu as pltpu
from jax.sharding import Mesh
from jax.sharding import PartitionSpec as P


HEAD_DIM = 128
CLUST_DEV = 8
SLOT = 8
SEQ = ("seq_0", "seq_1", "seq_2")
F32 = jnp.float32
BF16 = jnp.bfloat16


def shifted(array, by):
    count = lax.axis_size("head")
    return lax.ppermute(array, "head", [(i, (i + by) % count) for i in range(count)])


def in_hbm(array):
    return pltpu.with_memory_space_constraint(array, pltpu.HBM)


def params(**more):
    return pltpu.CompilerParams(vmem_limit_bytes=56 * 1024 * 1024, **more)


def first_blocks_kernel(where, own, left, right, w_own, w_left, w_right, out):
    total = jnp.dot(own[...], w_own[0], preferred_element_type=F32)
    total += jnp.dot(left[...], w_left[0], preferred_element_type=F32)
    total += jnp.dot(right[...], w_right[0], preferred_element_type=F32)
    out[0] = total


def first_blocks(where, own, left, right, weights):
    kinds, _, width = weights.shape
    rows, depth = own.shape
    whole = pl.BlockSpec((rows, depth), lambda j, w: (0, 0))
    return pl.pallas_call(
        first_blocks_kernel,
        out_shape=jax.ShapeDtypeStruct((kinds, rows, width), F32),
        grid_spec=pltpu.PrefetchScalarGridSpec(
            num_scalar_prefetch=1,
            grid=(kinds,),
            in_specs=[whole, whole, whole]
            + [pl.BlockSpec((1, depth, width), functools.partial(lambda b, j, w: (j, w[b], 0), b)) for b in range(3)],
            out_specs=pl.BlockSpec((1, rows, width), lambda j, w: (j, 0, 0)),
        ),
        compiler_params=params(),
        name="first_blocks",
    )(where, own, left, right, weights, weights, weights)


def pack_kernel(where, part, far_top, far_bottom, w_far, slot_of, out, projected):
    head = pl.program_id(0)
    kinds, rows, width = part.shape
    half = rows // 2
    heads = width // HEAD_DIM

    @pl.when(head == 0)
    def _():
        for kind in range(kinds):
            top = part[kind, :half] + jnp.dot(far_top[...], w_far[kind], preferred_element_type=F32)
            bottom = part[kind, half:] + jnp.dot(far_bottom[...], w_far[kind], preferred_element_type=F32)
            for h in range(heads):
                cols = slice(h * HEAD_DIM, (h + 1) * HEAD_DIM)
                to = slice(kind * HEAD_DIM, (kind + 1) * HEAD_DIM)
                projected[h, :half, to] = top[:, cols].astype(BF16)
                projected[h, half:, to] = bottom[:, cols].astype(BF16)

    rows_in = projected[head]
    slot_row = slot_of[0]
    devices, _, clusters, slot, lanes = out.shape
    step = 4
    chunk = step * clusters * slot

    def body(i, carry):
        iota = lax.broadcasted_iota(jnp.int32, (chunk, rows), 0) + i * chunk
        onehot = jnp.where(iota == slot_row, 1.0, 0.0).astype(BF16)
        packed = jnp.dot(onehot, rows_in, preferred_element_type=F32).astype(BF16)
        out[pl.ds(i * step, step), 0] = packed.reshape(step, clusters, slot, lanes)
        return carry

    lax.fori_loop(0, devices // step, body, 0, unroll=2)


def pack(where, part, far_top, far_bottom, weights, slot_index, devices, group, heads):
    kinds, rows, _ = part.shape
    width = heads * HEAD_DIM
    depth = far_top.shape[1]
    lanes = kinds * HEAD_DIM
    return pl.pallas_call(
        pack_kernel,
        out_shape=jax.ShapeDtypeStruct((devices, heads, CLUST_DEV, SLOT, lanes), BF16),
        grid_spec=pltpu.PrefetchScalarGridSpec(
            num_scalar_prefetch=1,
            grid=(heads,),
            in_specs=[
                pl.BlockSpec((kinds, rows, width), lambda h, w: (0, 0, group)),
                pl.BlockSpec((rows // 2, depth), lambda h, w: (0, 0)),
                pl.BlockSpec((rows // 2, depth), lambda h, w: (0, 0)),
                pl.BlockSpec((kinds, depth, width), lambda h, w: (0, w[3], group)),
                pl.BlockSpec((1, 1, rows), lambda h, w: (group * heads + h, 0, 0)),
            ],
            out_specs=pl.BlockSpec((devices, 1, CLUST_DEV, SLOT, lanes), lambda h, w: (0, h, 0, 0, 0)),
            scratch_shapes=[pltpu.VMEM((heads, rows, lanes), BF16)],
        ),
        compiler_params=params(),
        name="pack",
    )(where, part, far_top, far_bottom, weights, slot_index)


def attend_kernel(received, bias, out):
    devices, heads, _, slot, _ = received.shape
    bucket = devices * slot
    scale = 1.0 / math.sqrt(HEAD_DIM)
    rows = lax.broadcasted_iota(jnp.int32, (bucket, bucket), 0)
    cols = lax.broadcasted_iota(jnp.int32, (bucket, bucket), 1)
    causal = cols <= rows
    for h in range(heads):
        both = received[:, h, 0].reshape(bucket, 3 * HEAD_DIM)
        query, key, value = (both[:, i * HEAD_DIM : (i + 1) * HEAD_DIM] for i in range(3))
        scores = lax.dot_general(query, key, (((1,), (1,)), ((), ())), preferred_element_type=F32) * scale
        scores = jnp.where(causal & (bias[0, h : h + 1] > 0), scores, -1e30)
        row_max = jnp.max(scores, axis=-1, keepdims=True)
        exponentials = jnp.exp(scores - row_max)
        weights = (exponentials / jnp.sum(exponentials, axis=-1, keepdims=True)).astype(BF16)
        result = jnp.dot(weights, value, preferred_element_type=F32).astype(BF16)
        out[:, h, 0] = result.reshape(devices, slot, HEAD_DIM)


def attend(received, live):
    devices, heads, clusters, slot, lanes = received.shape
    bucket = devices * slot
    return pl.pallas_call(
        attend_kernel,
        out_shape=jax.ShapeDtypeStruct((devices, heads, clusters, slot, HEAD_DIM), BF16),
        grid=(clusters,),
        in_specs=[
            pl.BlockSpec((devices, heads, 1, slot, lanes), lambda c: (0, 0, c, 0, 0)),
            pl.BlockSpec((1, heads, bucket), lambda c: (c, 0, 0)),
        ],
        out_specs=pl.BlockSpec((devices, heads, 1, slot, HEAD_DIM), lambda c: (0, 0, c, 0, 0)),
        compiler_params=params(),
        name="attend",
    )(received, live)


def key_sums_kernel(keys, out):
    _, heads, _, _, width = keys.shape
    for h in range(heads):
        key = keys[:, h, 0].astype(F32)
        scaled = key * lax.rsqrt(jnp.mean(key * key, axis=-1, keepdims=True) + 1e-06)
        unit = (scaled / math.sqrt(width)).astype(BF16).astype(F32)
        out[0, h : h + 1] = jnp.sum(jnp.sum(unit, axis=0), axis=0, keepdims=True)


def key_sums(received):
    devices, heads, clusters, slot, _ = received.shape
    return pl.pallas_call(
        key_sums_kernel,
        out_shape=jax.ShapeDtypeStruct((clusters, heads, HEAD_DIM), F32),
        grid=(clusters,),
        in_specs=[pl.BlockSpec((devices, heads, 1, slot, HEAD_DIM), lambda c: (0, 0, c, 0, 1))],
        out_specs=pl.BlockSpec((1, heads, HEAD_DIM), lambda c: (c, 0, 0)),
        compiler_params=params(),
        name="key_sums",
    )(received)


def unpack_kernel(returned, slot_of, out):
    devices, _, clusters, slot, width = returned.shape
    slots = devices * clusters * slot
    rows = out.shape[0]
    source = returned[:, 0].reshape(slots, width)
    chunk = 256

    def body(i, carry):
        at = pl.ds(pl.multiple_of(i * chunk, chunk), chunk)
        iota = lax.broadcasted_iota(jnp.int32, (chunk, slots), 1)
        onehot = jnp.where(iota == slot_of[0, at], 1.0, 0.0).astype(BF16)
        out[at] = jnp.dot(onehot, source, preferred_element_type=F32).astype(BF16)
        return carry

    lax.fori_loop(0, rows // chunk, body, 0, unroll=2)


def unpack(returned, slot_index, group):
    devices, heads, clusters, slot, width = returned.shape
    rows = slot_index.shape[1]
    return pl.pallas_call(
        unpack_kernel,
        out_shape=jax.ShapeDtypeStruct((rows, heads * width), BF16),
        grid=(heads,),
        in_specs=[
            pl.BlockSpec((devices, 1, clusters, slot, width), lambda h: (0, h, 0, 0, 0)),
            pl.BlockSpec((1, rows, 1), lambda h: (group * heads + h, 0, 0)),
        ],
        out_specs=pl.BlockSpec((rows, width), lambda h: (0, h)),
        compiler_params=params(),
        name="unpack",
    )(returned, slot_index)


def local(tokens, project_weights, output_weights, cluster_ids):
    seq_count = lax.axis_size(SEQ)
    groups = lax.axis_size("head")
    here = lax.axis_index("head")
    width = output_weights.shape[0]
    heads = width // HEAD_DIM
    rows = tokens.shape[0]
    clusters = CLUST_DEV * seq_count

    assigned = cluster_ids[:, :, 0]
    matches = assigned[:, :, None] == jnp.arange(clusters, dtype=jnp.int32)
    counts = jnp.sum(matches.astype(jnp.int32), axis=1)
    row_iota = jnp.arange(rows, dtype=jnp.int32)
    earlier = (row_iota[None, :] < row_iota[:, None]).astype(BF16)
    before = jnp.einsum("ts,hsc->htc", earlier, matches.astype(BF16), preferred_element_type=F32)
    slot_rank = jnp.sum(jnp.where(matches, before, 0.0), axis=2).astype(jnp.int32)
    slot_index = assigned * SLOT + slot_rank

    by_owner = counts.T.reshape(seq_count, CLUST_DEV, heads)
    filled = lax.all_to_all(by_owner, SEQ, 0, 0, tiled=True)
    live = (filled.transpose(1, 2, 0)[..., None] > jnp.arange(SLOT, dtype=jnp.int32)).astype(F32)
    live = live.reshape(CLUST_DEV, heads, seq_count * SLOT)

    weights = project_weights.transpose(1, 0, 2)
    where = jnp.stack([here, (here - 1) % groups, (here + 1) % groups, (here + 2) % groups]).astype(jnp.int32)
    slot_rows, slot_cols = slot_index[:, None, :], slot_index[:, :, None]
    left, right = shifted(tokens, 1), shifted(tokens, -1)
    left, right, slot_rows, slot_cols, where = lax.optimization_barrier((left, right, slot_rows, slot_cols, where))
    half = rows // 2
    far_top, far_bottom = shifted(left[:half], 1), shifted(right[half:], -1)
    left, right = in_hbm(left), in_hbm(right)
    part = first_blocks(where, tokens, left, right, weights)

    out_weights, far_top, far_bottom = lax.optimization_barrier((output_weights, far_top, far_bottom))
    out_blocks = []
    for by in range(groups):
        block = lax.dynamic_slice(out_weights, (0, (here + by) % groups * width), (width, width))
        out_blocks.append(shifted(block, by) if by else block)

    chunks = 2
    some = heads // chunks
    received = []
    for chunk in range(chunks):
        packed = pack(where, part, in_hbm(far_top), in_hbm(far_bottom), weights, slot_rows, seq_count, chunk, some)
        arrived = lax.all_to_all(packed, SEQ, 0, 0, tiled=True)
        received.append(in_hbm(arrived))

    owned, gathered = [], []
    for chunk in range(chunks):
        buckets = attend(received[chunk], live[:, chunk * some : (chunk + 1) * some])
        owned.append(key_sums(received[chunk]))
        returned = lax.all_to_all(buckets, SEQ, 0, 0, tiled=True)
        attended = unpack(in_hbm(returned), slot_cols, chunk)
        gathered.append([attended] + [shifted(attended, by) for by in range(1, groups)])

    mixed = None
    for chunk in range(chunks):
        for by in (0, 1, 3, 2):
            depth = gathered[chunk][by].shape[1]
            share = out_blocks[by][chunk * depth : (chunk + 1) * depth]
            term = jnp.dot(gathered[chunk][by], share, preferred_element_type=F32)
            mixed = term if mixed is None else mixed + term
    owned = jnp.concatenate(owned, axis=1).transpose(1, 0, 2)
    return (mixed.astype(BF16), owned)


def solution(mesh):
    split = Mesh(
        mesh.devices.reshape(4, 4, 2, mesh.shape["head"]), ("seq_0", "seq_1", "seq_2", "head")
    )
    in_specs = (P(SEQ, "head"), P(None, None, "head"), P("head", None), P("head", SEQ, None))
    out_specs = (P(SEQ, "head"), P("head", SEQ, None))
    return jax.shard_map(local, mesh=split, in_specs=in_specs, out_specs=out_specs, check_vma=False)
```

```python
import functools
import math

import jax
import jax.numpy as jnp
from jax import lax
from jax.experimental import pallas as pl
from jax.experimental.pallas import tpu as pltpu
from jax.sharding import Mesh
from jax.sharding import PartitionSpec as P


HEAD_DIM = 128
CLUST_DEV = 8
SLOT = 8
SEQ = ("seq_0", "seq_1", "seq_2")
F32 = jnp.float32
BF16 = jnp.bfloat16
EMPTY = float(1 << 20)
FULL_BELOW = float(1 << 19)


def shifted(array, by):
    count = lax.axis_size("head")
    return lax.ppermute(array, "head", [(i, (i + by) % count) for i in range(count)])


def in_vmem(array):
    return pltpu.with_memory_space_constraint(array, pltpu.VMEM)


VMEM_WHOLE = pl.BlockSpec(memory_space=pltpu.VMEM)


def params():
    return pltpu.CompilerParams(vmem_limit_bytes=56 * 1024 * 1024)


def dot(a, b):
    return jnp.dot(a, b, preferred_element_type=F32)


def first_blocks_kernel(where, own, left_top, left_bottom, right_top, right_bottom, w_own, w_left, w_right, out):
    half = left_top.shape[0]
    for part, left, right in ((slice(0, half), left_top, right_top), (slice(half, None), left_bottom, right_bottom)):
        total = dot(own[part], w_own[0])
        total += dot(left[...], w_left[0])
        total += dot(right[...], w_right[0])
        out[0, part] = total


def first_blocks(where, own, halves, weights):
    kinds, _, width = weights.shape
    rows, depth = own.shape
    return pl.pallas_call(
        first_blocks_kernel,
        out_shape=jax.ShapeDtypeStruct((kinds, rows, width), F32),
        grid_spec=pltpu.PrefetchScalarGridSpec(
            num_scalar_prefetch=1,
            grid=(kinds,),
            in_specs=[pl.BlockSpec((rows, depth), lambda j, w: (0, 0))]
            + [VMEM_WHOLE] * 4
            + [pl.BlockSpec((1, depth, width), functools.partial(lambda b, j, w: (j, w[b], 0), b)) for b in range(3)],
            out_specs=pl.BlockSpec((1, rows, width), lambda j, w: (j, 0, 0)),
        ),
        compiler_params=params(),
        name="first_blocks",
    )(where, own, *[in_vmem(half) for half in halves], weights, weights, weights)


def pack_kernel(where, part, far_top, far_bottom, w_far, slot_of, out, projected):
    head = pl.program_id(0)
    kinds, rows, _ = part.shape
    half = rows // 2
    heads = projected.shape[0]

    @pl.when(head == 0)
    def _():
        for kind in range(kinds):
            to = slice(kind * HEAD_DIM, (kind + 1) * HEAD_DIM)
            for at, far in ((slice(0, half), far_top), (slice(half, rows), far_bottom)):
                done = (part[kind, at] + dot(far[...], w_far[kind])).astype(BF16)
                for h in range(heads):
                    projected[h, at, to] = done[:, h * HEAD_DIM : (h + 1) * HEAD_DIM]
        for h in range(heads):
            projected[h, :, kinds * HEAD_DIM :] = jnp.ones((rows, HEAD_DIM), BF16)

    rows_in = projected[head]
    slot_row = slot_of[0]
    devices, _, clusters, slot, _ = out.shape
    step = 4
    chunk = step * clusters * slot

    def body(i, carry):
        iota = lax.broadcasted_iota(jnp.int32, (chunk, rows), 0) + i * chunk
        onehot = jnp.where(iota == slot_row, 1.0, 0.0).astype(BF16)
        packed = dot(onehot, rows_in)
        at = pl.ds(i * step, step)
        for kind in range(kinds):
            block = packed[:, kind * HEAD_DIM : (kind + 1) * HEAD_DIM]
            if kind == 1:
                block = block + (EMPTY - EMPTY * packed[:, kinds * HEAD_DIM :])
            block = block.astype(BF16).reshape(step, clusters, slot, HEAD_DIM)
            out[at, 0, :, :, kind * HEAD_DIM : (kind + 1) * HEAD_DIM] = block
        return carry

    lax.fori_loop(0, devices // step, body, 0, unroll=2)


def pack(where, part, far_top, far_bottom, weights, slot_rows, devices, group, heads):
    kinds = weights.shape[0]
    rows = slot_rows.shape[2]
    width = heads * HEAD_DIM
    depth = far_top.shape[1]
    lanes = kinds * HEAD_DIM
    return pl.pallas_call(
        pack_kernel,
        out_shape=jax.ShapeDtypeStruct((devices, heads, CLUST_DEV, SLOT, lanes), BF16),
        grid_spec=pltpu.PrefetchScalarGridSpec(
            num_scalar_prefetch=1,
            grid=(heads,),
            in_specs=[
                pl.BlockSpec((kinds, rows, width), lambda h, w: (0, 0, group)),
                VMEM_WHOLE,
                VMEM_WHOLE,
                pl.BlockSpec((kinds, depth, width), lambda h, w: (0, w[3], group)),
                pl.BlockSpec((1, 1, rows), lambda h, w: (group * heads + h, 0, 0)),
            ],
            out_specs=pl.BlockSpec((devices, 1, CLUST_DEV, SLOT, lanes), lambda h, w: (0, h, 0, 0, 0)),
            scratch_shapes=[pltpu.VMEM((heads, rows, lanes + HEAD_DIM), BF16)],
        ),
        compiler_params=params(),
        name="pack",
    )(where, part, in_vmem(far_top), in_vmem(far_bottom), weights, slot_rows)


def attend_kernel(streamed, received, out, sums):
    devices, heads, _, slot, _ = received.shape
    bucket = devices * slot
    together = out.shape[2]
    scale = 1.0 / math.sqrt(HEAD_DIM)
    rows = lax.broadcasted_iota(jnp.int32, (bucket, bucket), 0)
    cols = lax.broadcasted_iota(jnp.int32, (bucket, bucket), 1)
    causal = cols <= rows
    first_lane = jnp.where(lax.broadcasted_iota(jnp.int32, (16, HEAD_DIM), 1) == 0, 1.0, 0.0).astype(BF16)
    for c in range(together):
        for h in range(heads):
            both = received[:, h, c if streamed else pl.program_id(0) * together + c].reshape(bucket, 3 * HEAD_DIM)
            query, key, value = (both[:, i * HEAD_DIM : (i + 1) * HEAD_DIM] for i in range(3))
            query = jnp.concatenate([query, first_lane], axis=0)
            product = lax.dot_general(query, key, (((1,), (1,)), ((), ())), preferred_element_type=F32)
            filled = product[bucket : bucket + 1] < FULL_BELOW
            scores = jnp.where(causal & filled, product[:bucket] * scale, -1e30)
            row_max = jnp.max(scores, axis=-1, keepdims=True)
            exponentials = jnp.exp(scores - row_max)
            weights = (exponentials / jnp.sum(exponentials, axis=-1, keepdims=True)).astype(BF16)
            out[:, h, c] = dot(weights, value).astype(BF16).reshape(devices, slot, HEAD_DIM)

            key = key.astype(F32)
            scaled = key * lax.rsqrt(jnp.mean(key * key, axis=-1, keepdims=True) + 1e-06)
            unit = (scaled / math.sqrt(HEAD_DIM)).astype(BF16).astype(F32)
            unit = jnp.where(key < FULL_BELOW, unit, 0.0)
            sums[c, h : h + 1] = jnp.sum(unit, axis=0, keepdims=True)


def attend(received, streamed):
    devices, heads, clusters, slot, _ = received.shape
    together = 2
    block = pl.BlockSpec((devices, heads, together, slot, 3 * HEAD_DIM), lambda c: (0, 0, c, 0, 0))
    return pl.pallas_call(
        functools.partial(attend_kernel, streamed),
        out_shape=(
            jax.ShapeDtypeStruct((devices, heads, clusters, slot, HEAD_DIM), BF16),
            jax.ShapeDtypeStruct((clusters, heads, HEAD_DIM), F32),
        ),
        grid=(clusters // together,),
        in_specs=[block if streamed else VMEM_WHOLE],
        out_specs=(
            pl.BlockSpec((devices, heads, together, slot, HEAD_DIM), lambda c: (0, 0, c, 0, 0)),
            pl.BlockSpec((together, heads, HEAD_DIM), lambda c: (c, 0, 0)),
        ),
        compiler_params=params(),
        name="attend",
    )(received if streamed else in_vmem(received))


def unpack_kernel(returned, slot_of, out):
    devices, _, clusters, slot, width = returned.shape
    slots = devices * clusters * slot
    rows = out.shape[0]
    source = returned[:, pl.program_id(0)].reshape(slots, width)
    chunk = 256

    def body(i, carry):
        at = pl.ds(pl.multiple_of(i * chunk, chunk), chunk)
        iota = lax.broadcasted_iota(jnp.int32, (chunk, slots), 1)
        onehot = jnp.where(iota == slot_of[0, at], 1.0, 0.0).astype(BF16)
        out[at] = dot(onehot, source).astype(BF16)
        return carry

    lax.fori_loop(0, rows // chunk, body, 0, unroll=2)


def unpack(returned, slot_cols, group):
    _, heads, _, _, width = returned.shape
    rows = slot_cols.shape[1]
    return pl.pallas_call(
        unpack_kernel,
        out_shape=jax.ShapeDtypeStruct((rows, heads * width), BF16),
        grid=(heads,),
        in_specs=[VMEM_WHOLE, pl.BlockSpec((1, rows, 1), lambda h: (group * heads + h, 0, 0))],
        out_specs=pl.BlockSpec((rows, width), lambda h: (0, h)),
        compiler_params=params(),
        name="unpack",
    )(in_vmem(returned), slot_cols)


def near_kernel(count, *refs):
    blocks, weights, out = refs[:count], refs[count : 2 * count], refs[-1]
    total = dot(blocks[0][...], weights[0][...])
    for block, weight in zip(blocks[1:], weights[1:]):
        total += dot(block[...], weight[...])
    out[...] = total


def finish_kernel(count, *refs):
    near, blocks, weights, out = refs[0], refs[1 : count + 1], refs[count + 1 : 2 * count + 1], refs[-1]
    rows = out.shape[0]
    at = pl.ds(pl.multiple_of(pl.program_id(0) * rows, rows), rows)
    total = near[at]
    for block, weight in zip(blocks, weights):
        total += dot(block[at], weight[...])
    out[...] = total.astype(BF16)


def weight_spec(chunk, depth, width):
    return pl.BlockSpec((depth, width), lambda *_: (chunk, 0))


def near_products(parts, rows, width):
    blocks = [in_vmem(block) for block, _, _ in parts]
    return pl.pallas_call(
        functools.partial(near_kernel, len(parts)),
        out_shape=jax.ShapeDtypeStruct((rows, width), F32),
        grid=(1,),
        in_specs=[VMEM_WHOLE] * len(parts) + [weight_spec(c, b.shape[1], width) for b, _, c in parts],
        out_specs=pl.BlockSpec((rows, width), lambda i: (0, 0)),
        compiler_params=params(),
        name="near_products",
    )(*blocks, *[w for _, w, _ in parts])


def finish(near, parts, rows, width):
    blocks = [in_vmem(block) for block, _, _ in parts]
    steps = 4
    return pl.pallas_call(
        functools.partial(finish_kernel, len(parts)),
        out_shape=jax.ShapeDtypeStruct((rows, width), BF16),
        grid=(steps,),
        in_specs=[VMEM_WHOLE] * (1 + len(parts)) + [weight_spec(c, b.shape[1], width) for b, _, c in parts],
        out_specs=pl.BlockSpec((rows // steps, width), lambda i: (i, 0)),
        compiler_params=params(),
        name="finish",
    )(in_vmem(near), *blocks, *[w for _, w, _ in parts])


def local(tokens, project_weights, output_weights, cluster_ids):
    seq_count = lax.axis_size(SEQ)
    groups = lax.axis_size("head")
    here = lax.axis_index("head")
    width = output_weights.shape[0]
    heads = width // HEAD_DIM
    rows = tokens.shape[0]
    half = rows // 2
    clusters = CLUST_DEV * seq_count

    assigned = cluster_ids[:, :, 0]
    matches = assigned[:, :, None] == jnp.arange(clusters, dtype=jnp.int32)
    row_iota = jnp.arange(rows, dtype=jnp.int32)
    earlier = (row_iota[None, :] < row_iota[:, None]).astype(BF16)
    before = jnp.einsum("ts,hsc->htc", earlier, matches.astype(BF16), preferred_element_type=F32)
    slot_rank = jnp.sum(jnp.where(matches, before, 0.0), axis=2).astype(jnp.int32)
    slot_index = assigned * SLOT + slot_rank
    slot_rows, slot_cols = slot_index[:, None, :], slot_index[:, :, None]

    weights = project_weights.transpose(1, 0, 2)
    where = jnp.stack([here, (here - 1) % groups, (here + 1) % groups, (here + 2) % groups]).astype(jnp.int32)

    top, bottom = tokens[:half], tokens[half:]
    left_top, right_bottom = shifted(top, 1), shifted(bottom, -1)
    left_bottom, right_top = shifted(bottom, 1), shifted(top, -1)
    left_top, right_bottom, slot_rows, slot_cols, where = lax.optimization_barrier(
        (left_top, right_bottom, slot_rows, slot_cols, where)
    )
    far_top, far_bottom = shifted(left_top, 1), shifted(right_bottom, -1)
    part = first_blocks(where, tokens, (left_top, left_bottom, right_top, right_bottom), weights)

    out_weights, far_top, far_bottom = lax.optimization_barrier((output_weights, far_top, far_bottom))
    out_blocks = []
    for by in range(groups):
        block = lax.dynamic_slice(out_weights, (0, (here + by) % groups * width), (width, width))
        out_blocks.append(shifted(block, by) if by else block)

    chunks = 2
    some = heads // chunks
    received = []
    for chunk in range(chunks):
        packed = pack(where, part, far_top, far_bottom, weights, slot_rows, seq_count, chunk, some)
        received.append(lax.all_to_all(packed, SEQ, 0, 0, tiled=True))

    owned, gathered = [], []
    for chunk in range(chunks):
        buckets, sums = attend(received[chunk], streamed=chunk == 0)
        owned.append(sums)
        returned = lax.all_to_all(buckets, SEQ, 0, 0, tiled=True)
        attended = unpack(returned, slot_cols, chunk)
        gathered.append([attended] + [shifted(attended, by) for by in range(1, groups)])

    parts = [(gathered[chunk][by], out_blocks[by], chunk) for chunk in range(chunks) for by in range(groups)]
    near = near_products(parts[: groups + 1], rows, width)
    mixed = finish(near, parts[groups + 1 :], rows, width)
    owned = jnp.concatenate(owned, axis=1).transpose(1, 0, 2)
    return (mixed, owned)


def solution(mesh):
    split = Mesh(
        mesh.devices.reshape(4, 4, 2, mesh.shape["head"]), ("seq_0", "seq_1", "seq_2", "head")
    )
    in_specs = (P(SEQ, "head"), P(None, None, "head"), P("head", None), P("head", SEQ, None))
    out_specs = (P(SEQ, "head"), P("head", SEQ, None))
    return jax.shard_map(local, mesh=split, in_specs=in_specs, out_specs=out_specs, check_vma=False)
```

```python
import functools
import math

import jax
import jax.numpy as jnp
from jax import lax
from jax.experimental import pallas as pl
from jax.experimental.pallas import tpu as pltpu
from jax.sharding import Mesh
from jax.sharding import PartitionSpec as P


HEAD_DIM = 128
CLUST_DEV = 8
SLOT = 8
SEQ = ("seq_0", "seq_1", "seq_2")
F32 = jnp.float32
BF16 = jnp.bfloat16
EMPTY = float(1 << 20)
FULL_BELOW = float(1 << 19)


def shifted(array, by):
    count = lax.axis_size("head")
    return lax.ppermute(array, "head", [(i, (i + by) % count) for i in range(count)])


def in_vmem(array):
    return pltpu.with_memory_space_constraint(array, pltpu.VMEM)


VMEM_WHOLE = pl.BlockSpec(memory_space=pltpu.VMEM)


def params():
    return pltpu.CompilerParams(vmem_limit_bytes=56 * 1024 * 1024)


def dot(a, b):
    return jnp.dot(a, b, preferred_element_type=F32)


def first_blocks_kernel(where, own, left_top, left_bottom, right_top, right_bottom, w_own, w_left, w_right, out):
    half = left_top.shape[0]
    for part, left, right in ((slice(0, half), left_top, right_top), (slice(half, None), left_bottom, right_bottom)):
        total = dot(own[part], w_own[0])
        total += dot(left[...], w_left[0])
        total += dot(right[...], w_right[0])
        out[0, part] = total


def first_blocks(where, own, halves, weights):
    kinds, _, width = weights.shape
    rows, depth = own.shape
    return pl.pallas_call(
        first_blocks_kernel,
        out_shape=jax.ShapeDtypeStruct((kinds, rows, width), F32),
        grid_spec=pltpu.PrefetchScalarGridSpec(
            num_scalar_prefetch=1,
            grid=(kinds,),
            in_specs=[pl.BlockSpec((rows, depth), lambda j, w: (0, 0))]
            + [VMEM_WHOLE] * 4
            + [pl.BlockSpec((1, depth, width), functools.partial(lambda b, j, w: (j, w[b], 0), b)) for b in range(3)],
            out_specs=pl.BlockSpec((1, rows, width), lambda j, w: (j, 0, 0)),
        ),
        compiler_params=params(),
        name="first_blocks",
    )(where, own, *[in_vmem(half) for half in halves], weights, weights, weights)


def pack_kernel(where, part, far_top, far_bottom, w_far, slot_of, out, projected):
    head = pl.program_id(0)
    kinds, rows, _ = part.shape
    half = rows // 2
    heads = projected.shape[0]

    @pl.when(head == 0)
    def _():
        for kind in range(kinds):
            to = slice(kind * HEAD_DIM, (kind + 1) * HEAD_DIM)
            for at, far in ((slice(0, half), far_top), (slice(half, rows), far_bottom)):
                done = (part[kind, at] + dot(far[...], w_far[kind])).astype(BF16)
                for h in range(heads):
                    projected[h, at, to] = done[:, h * HEAD_DIM : (h + 1) * HEAD_DIM]
        for h in range(heads):
            projected[h, :, kinds * HEAD_DIM :] = jnp.ones((rows, HEAD_DIM), BF16)

    rows_in = projected[head]
    slot_row = slot_of[0]
    devices, _, clusters, slot, _ = out.shape
    step = 4
    chunk = step * clusters * slot

    def body(i, carry):
        iota = lax.broadcasted_iota(jnp.int32, (chunk, rows), 0) + i * chunk
        onehot = jnp.where(iota == slot_row, 1.0, 0.0).astype(BF16)
        packed = dot(onehot, rows_in)
        at = pl.ds(i * step, step)
        for kind in range(kinds):
            block = packed[:, kind * HEAD_DIM : (kind + 1) * HEAD_DIM]
            if kind == 1:
                block = block + (EMPTY - EMPTY * packed[:, kinds * HEAD_DIM :])
            block = block.astype(BF16).reshape(step, clusters, slot, HEAD_DIM)
            out[at, 0, :, :, kind * HEAD_DIM : (kind + 1) * HEAD_DIM] = block
        return carry

    lax.fori_loop(0, devices // step, body, 0, unroll=2)


def pack(where, part, far_top, far_bottom, weights, slot_rows, devices, group, heads):
    kinds = weights.shape[0]
    rows = slot_rows.shape[2]
    width = heads * HEAD_DIM
    depth = far_top.shape[1]
    lanes = kinds * HEAD_DIM
    return pl.pallas_call(
        pack_kernel,
        out_shape=jax.ShapeDtypeStruct((devices, heads, CLUST_DEV, SLOT, lanes), BF16),
        grid_spec=pltpu.PrefetchScalarGridSpec(
            num_scalar_prefetch=1,
            grid=(heads,),
            in_specs=[
                pl.BlockSpec((kinds, rows, width), lambda h, w: (0, 0, group)),
                VMEM_WHOLE,
                VMEM_WHOLE,
                pl.BlockSpec((kinds, depth, width), lambda h, w: (0, w[3], group)),
                pl.BlockSpec((1, 1, rows), lambda h, w: (group * heads + h, 0, 0)),
            ],
            out_specs=pl.BlockSpec((devices, 1, CLUST_DEV, SLOT, lanes), lambda h, w: (0, h, 0, 0, 0)),
            scratch_shapes=[pltpu.VMEM((heads, rows, lanes + HEAD_DIM), BF16)],
        ),
        compiler_params=params(),
        name="pack",
    )(where, part, in_vmem(far_top), in_vmem(far_bottom), weights, slot_rows)


def attend_kernel(streamed, received, out, sums):
    devices, heads, _, slot, _ = received.shape
    bucket = devices * slot
    together = out.shape[2]
    scale = 1.0 / math.sqrt(HEAD_DIM)
    rows = lax.broadcasted_iota(jnp.int32, (bucket, bucket), 0)
    cols = lax.broadcasted_iota(jnp.int32, (bucket, bucket), 1)
    causal = cols <= rows
    first_lane = jnp.where(lax.broadcasted_iota(jnp.int32, (16, HEAD_DIM), 1) == 0, 1.0, 0.0).astype(BF16)
    for c in range(together):
        for h in range(heads):
            both = received[:, h, c if streamed else pl.program_id(0) * together + c].reshape(bucket, 3 * HEAD_DIM)
            query, key, value = (both[:, i * HEAD_DIM : (i + 1) * HEAD_DIM] for i in range(3))
            query = jnp.concatenate([query, first_lane], axis=0)
            product = lax.dot_general(query, key, (((1,), (1,)), ((), ())), preferred_element_type=F32)
            filled = product[bucket : bucket + 1] < FULL_BELOW
            scores = jnp.where(causal & filled, product[:bucket] * scale, -1e30)
            row_max = jnp.max(scores, axis=-1, keepdims=True)
            exponentials = jnp.exp(scores - row_max)
            weights = (exponentials / jnp.sum(exponentials, axis=-1, keepdims=True)).astype(BF16)
            out[:, h, c] = dot(weights, value).astype(BF16).reshape(devices, slot, HEAD_DIM)

            key = key.astype(F32)
            scaled = key * lax.rsqrt(jnp.mean(key * key, axis=-1, keepdims=True) + 1e-06)
            unit = (scaled / math.sqrt(HEAD_DIM)).astype(BF16).astype(F32)
            unit = jnp.where(key < FULL_BELOW, unit, 0.0)
            sums[c, h : h + 1] = jnp.sum(unit, axis=0, keepdims=True)


def attend(received, streamed):
    devices, heads, clusters, slot, _ = received.shape
    together = 2
    block = pl.BlockSpec((devices, heads, together, slot, 3 * HEAD_DIM), lambda c: (0, 0, c, 0, 0))
    return pl.pallas_call(
        functools.partial(attend_kernel, streamed),
        out_shape=(
            jax.ShapeDtypeStruct((devices, heads, clusters, slot, HEAD_DIM), BF16),
            jax.ShapeDtypeStruct((clusters, heads, HEAD_DIM), F32),
        ),
        grid=(clusters // together,),
        in_specs=[block if streamed else VMEM_WHOLE],
        out_specs=(
            pl.BlockSpec((devices, heads, together, slot, HEAD_DIM), lambda c: (0, 0, c, 0, 0)),
            pl.BlockSpec((together, heads, HEAD_DIM), lambda c: (c, 0, 0)),
        ),
        compiler_params=params(),
        name="attend",
    )(received if streamed else in_vmem(received))


def unpack_kernel(returned, slot_of, top, bottom):
    devices, _, clusters, slot, width = returned.shape
    slots = devices * clusters * slot
    half = top.shape[0]
    source = returned[:, pl.program_id(0)].reshape(slots, width)
    chunk = 256

    iota = lax.broadcasted_iota(jnp.int32, (chunk, slots), 1)
    for start in range(0, 2 * half, chunk):
        onehot = jnp.where(iota == slot_of[0, start : start + chunk], 1.0, 0.0).astype(BF16)
        out, to = (top, start) if start < half else (bottom, start - half)
        out[to : to + chunk] = dot(onehot, source).astype(BF16)


def unpack(returned, slot_cols, group):
    _, heads, _, _, width = returned.shape
    rows = slot_cols.shape[1]
    return pl.pallas_call(
        unpack_kernel,
        out_shape=(jax.ShapeDtypeStruct((rows // 2, heads * width), BF16),) * 2,
        grid=(heads,),
        in_specs=[VMEM_WHOLE, pl.BlockSpec((1, rows, 1), lambda h: (group * heads + h, 0, 0))],
        out_specs=(pl.BlockSpec((rows // 2, width), lambda h: (0, h)),) * 2,
        compiler_params=params(),
        name="unpack",
    )(in_vmem(returned), slot_cols)


def products_kernel(count, carried, *refs):
    pairs, weights = refs[carried : carried + 2 * count], refs[carried + 2 * count : carried + 3 * count]
    out = refs[-1]

    def add(side):
        total = refs[0][...] if carried else 0.0
        for k in range(count):
            total += dot(pairs[2 * k + side][...], weights[k][...])
        out[...] = total.astype(out.dtype)

    pl.when(pl.program_id(0) == 0)(lambda: add(0))
    pl.when(pl.program_id(0) == 1)(lambda: add(1))


def products(total, parts, chunk, kind):
    half, depth = parts[0][0].shape
    width = parts[0][2].shape[1]
    block = pl.BlockSpec((half, width), lambda i: (i, 0))
    carried = [] if total is None else [total]
    return pl.pallas_call(
        functools.partial(products_kernel, len(parts), len(carried)),
        out_shape=jax.ShapeDtypeStruct((2 * half, width), kind),
        grid=(2,),
        in_specs=[block] * len(carried)
        + [VMEM_WHOLE] * (2 * len(parts))
        + [pl.BlockSpec((depth, width), lambda i: (chunk, 0))] * len(parts),
        out_specs=block,
        compiler_params=params(),
        name="products",
    )(*carried, *[in_vmem(side) for part in parts for side in part[:2]], *[part[2] for part in parts])


def local(tokens, project_weights, output_weights, cluster_ids):
    seq_count = lax.axis_size(SEQ)
    groups = lax.axis_size("head")
    here = lax.axis_index("head")
    width = output_weights.shape[0]
    heads = width // HEAD_DIM
    rows = tokens.shape[0]
    half = rows // 2
    clusters = CLUST_DEV * seq_count

    assigned = cluster_ids[:, :, 0]
    matches = assigned[:, :, None] == jnp.arange(clusters, dtype=jnp.int32)
    row_iota = jnp.arange(rows, dtype=jnp.int32)
    earlier = (row_iota[None, :] < row_iota[:, None]).astype(BF16)
    before = jnp.einsum("ts,hsc->htc", earlier, matches.astype(BF16), preferred_element_type=F32)
    slot_rank = jnp.sum(jnp.where(matches, before, 0.0), axis=2).astype(jnp.int32)
    slot_index = assigned * SLOT + slot_rank
    slot_rows, slot_cols = slot_index[:, None, :], slot_index[:, :, None]

    weights = project_weights.transpose(1, 0, 2)
    where = jnp.stack([here, (here - 1) % groups, (here + 1) % groups, (here + 2) % groups]).astype(jnp.int32)

    top, bottom = tokens[:half], tokens[half:]
    left_top, right_bottom = shifted(top, 1), shifted(bottom, -1)
    left_bottom, right_top = shifted(bottom, 1), shifted(top, -1)
    left_top, right_bottom, slot_rows, slot_cols, where = lax.optimization_barrier(
        (left_top, right_bottom, slot_rows, slot_cols, where)
    )
    far_top, far_bottom = shifted(left_top, 1), shifted(right_bottom, -1)
    part = first_blocks(where, tokens, (left_top, left_bottom, right_top, right_bottom), weights)

    out_weights, far_top, far_bottom = lax.optimization_barrier((output_weights, far_top, far_bottom))
    out_blocks = []
    for by in range(groups):
        block = lax.dynamic_slice(out_weights, (0, (here + by) % groups * width), (width, width))
        out_blocks.append(shifted(block, by) if by else block)

    chunks = 2
    some = heads // chunks
    received = []
    for chunk in range(chunks):
        packed = pack(where, part, far_top, far_bottom, weights, slot_rows, seq_count, chunk, some)
        received.append(lax.all_to_all(packed, SEQ, 0, 0, tiled=True))

    owned, gathered = [], []
    for chunk in range(chunks):
        buckets, sums = attend(received[chunk], streamed=chunk == 0)
        owned.append(sums)
        returned = lax.all_to_all(buckets, SEQ, 0, 0, tiled=True)
        top, bottom = unpack(returned, slot_cols, chunk)
        left_top, right_bottom = shifted(top, 1), shifted(bottom, -1)
        left_bottom, right_top = shifted(bottom, 1), shifted(top, -1)
        far_top, far_bottom = shifted(left_top, 1), shifted(right_bottom, -1)
        gathered.append(((top, bottom), (left_top, left_bottom), (far_top, far_bottom), (right_top, right_bottom)))

    total = None
    for chunk in range(chunks):
        parts = [(*gathered[chunk][by], out_blocks[by]) for by in range(groups)]
        last = chunk == chunks - 1
        total = products(total, parts[:2] + parts[3:], chunk, F32)
        total = products(total, parts[2:3], chunk, BF16 if last else F32)
    owned = jnp.concatenate(owned, axis=1).transpose(1, 0, 2)
    return (total, owned)


def solution(mesh):
    split = Mesh(
        mesh.devices.reshape(4, 4, 2, mesh.shape["head"]), ("seq_0", "seq_1", "seq_2", "head")
    )
    in_specs = (P(SEQ, "head"), P(None, None, "head"), P("head", None), P("head", SEQ, None))
    out_specs = (P(SEQ, "head"), P("head", SEQ, None))
    return jax.shard_map(local, mesh=split, in_specs=in_specs, out_specs=out_specs, check_vma=False)
```

```python
import functools
import math

import jax
import jax.numpy as jnp
from jax import lax
from jax.experimental import pallas as pl
from jax.experimental.pallas import tpu as pltpu
from jax.sharding import Mesh
from jax.sharding import PartitionSpec as P


HEAD_DIM = 128
CLUST_DEV = 8
SLOT = 8
SEQ = ("seq_0", "seq_1", "seq_2")
F32 = jnp.float32
BF16 = jnp.bfloat16
EMPTY = float(1 << 20)
FULL_BELOW = float(1 << 19)

TURNS = tuple((dz, dc) for dz in range(4) for dc in range(2))


def shifted(array, by):
    count = lax.axis_size("head")
    return lax.ppermute(array, "head", [(i, (i + by) % count) for i in range(count)])


def in_vmem(array):
    return pltpu.with_memory_space_constraint(array, pltpu.VMEM)


VMEM_WHOLE = pl.BlockSpec(memory_space=pltpu.VMEM)


def params():
    return pltpu.CompilerParams(vmem_limit_bytes=56 * 1024 * 1024)


def dot(a, b):
    return jnp.dot(a, b, preferred_element_type=F32)


def first_blocks_kernel(where, own, left_top, left_bottom, right_top, right_bottom, w_own, w_left, w_right, out):
    half = left_top.shape[0]
    for part, left, right in ((slice(0, half), left_top, right_top), (slice(half, None), left_bottom, right_bottom)):
        total = dot(own[part], w_own[0])
        total += dot(left[...], w_left[0])
        total += dot(right[...], w_right[0])
        out[0, part] = total


def first_blocks(where, own, halves, weights):
    kinds, _, width = weights.shape
    rows, depth = own.shape
    return pl.pallas_call(
        first_blocks_kernel,
        out_shape=jax.ShapeDtypeStruct((kinds, rows, width), F32),
        grid_spec=pltpu.PrefetchScalarGridSpec(
            num_scalar_prefetch=1,
            grid=(kinds,),
            in_specs=[pl.BlockSpec((rows, depth), lambda j, w: (0, 0))]
            + [VMEM_WHOLE] * 4
            + [pl.BlockSpec((1, depth, width), functools.partial(lambda b, j, w: (j, w[b], 0), b)) for b in range(3)],
            out_specs=pl.BlockSpec((1, rows, width), lambda j, w: (j, 0, 0)),
        ),
        compiler_params=params(),
        name="first_blocks",
    )(where, own, *[in_vmem(half) for half in halves], weights, weights, weights)


def pack_kernel(where, part, far_top, far_bottom, w_far, slot_of, out, projected):
    head = pl.program_id(0)
    kinds, rows, _ = part.shape
    half = rows // 2
    heads = projected.shape[0]

    @pl.when(head == 0)
    def _():
        for kind in range(kinds):
            to = slice(kind * HEAD_DIM, (kind + 1) * HEAD_DIM)
            for at, far in ((slice(0, half), far_top), (slice(half, rows), far_bottom)):
                done = (part[kind, at] + dot(far[...], w_far[kind])).astype(BF16)
                for h in range(heads):
                    projected[h, at, to] = done[:, h * HEAD_DIM : (h + 1) * HEAD_DIM]
        for h in range(heads):
            projected[h, :, kinds * HEAD_DIM :] = jnp.ones((rows, HEAD_DIM), BF16)

    rows_in = projected[head]
    slot_row = slot_of[0]
    devices, _, clusters, slot, _ = out.shape
    step = 4
    chunk = step * clusters * slot

    def body(i, carry):
        iota = lax.broadcasted_iota(jnp.int32, (chunk, rows), 0) + i * chunk
        onehot = jnp.where(iota == slot_row, 1.0, 0.0).astype(BF16)
        packed = dot(onehot, rows_in)
        at = pl.ds(i * step, step)
        for kind in range(kinds):
            block = packed[:, kind * HEAD_DIM : (kind + 1) * HEAD_DIM]
            if kind == 1:
                block = block + (EMPTY - EMPTY * packed[:, kinds * HEAD_DIM :])
            block = block.astype(BF16).reshape(step, clusters, slot, HEAD_DIM)
            out[at, 0, :, :, kind * HEAD_DIM : (kind + 1) * HEAD_DIM] = block
        return carry

    lax.fori_loop(0, devices // step, body, 0, unroll=2)


def pack(where, part, far_top, far_bottom, weights, slot_rows, devices, group, heads):
    kinds = weights.shape[0]
    rows = slot_rows.shape[2]
    width = heads * HEAD_DIM
    depth = far_top.shape[1]
    lanes = kinds * HEAD_DIM
    return pl.pallas_call(
        pack_kernel,
        out_shape=jax.ShapeDtypeStruct((devices, heads, CLUST_DEV, SLOT, lanes), BF16),
        grid_spec=pltpu.PrefetchScalarGridSpec(
            num_scalar_prefetch=1,
            grid=(heads,),
            in_specs=[
                pl.BlockSpec((kinds, rows, width), lambda h, w: (0, 0, group)),
                VMEM_WHOLE,
                VMEM_WHOLE,
                pl.BlockSpec((kinds, depth, width), lambda h, w: (0, w[3], group)),
                pl.BlockSpec((1, 1, rows), lambda h, w: (group * heads + h, 0, 0)),
            ],
            out_specs=pl.BlockSpec((devices, 1, CLUST_DEV, SLOT, lanes), lambda h, w: (0, h, 0, 0, 0)),
            scratch_shapes=[pltpu.VMEM((heads, rows, lanes + HEAD_DIM), BF16)],
        ),
        compiler_params=params(),
        name="pack",
    )(where, part, in_vmem(far_top), in_vmem(far_bottom), weights, slot_rows)


def attend_kernel(outputs, streamed, turn, received, *outs):
    outs, sums = outs[:outputs], outs[outputs]
    spans, within, heads, _, slot, _ = received.shape
    span = within * slot
    bucket = spans * span
    together = outs[0].shape[2]
    first = turn[0] if outputs > 1 else 0
    scale = 1.0 / math.sqrt(HEAD_DIM)
    rows = (lax.broadcasted_iota(jnp.int32, (bucket, bucket), 0) + first * span) & (bucket - 1)
    cols = lax.broadcasted_iota(jnp.int32, (bucket, bucket), 1)
    causal = cols <= rows
    first_lane = jnp.where(lax.broadcasted_iota(jnp.int32, (16, HEAD_DIM), 1) == 0, 1.0, 0.0).astype(BF16)
    for c in range(together):
        at = c if streamed else pl.program_id(0) * together + c
        for h in range(heads):
            key, value = (
                received[:, :, h, at, :, i * HEAD_DIM : (i + 1) * HEAD_DIM].reshape(bucket, HEAD_DIM) for i in (1, 2)
            )
            if outputs > 1:
                query = [
                    received[(first + k) & (spans - 1), :, h, at, :, :HEAD_DIM].reshape(span, HEAD_DIM)
                    for k in range(spans)
                ]
            else:
                query = [received[:, :, h, at, :, :HEAD_DIM].reshape(bucket, HEAD_DIM)]
            query = jnp.concatenate([*query, first_lane], axis=0)
            product = lax.dot_general(query, key, (((1,), (1,)), ((), ())), preferred_element_type=F32)
            filled = product[bucket : bucket + 1] < FULL_BELOW
            scores = jnp.where(causal & filled, product[:bucket] * scale, -1e30)
            row_max = jnp.max(scores, axis=-1, keepdims=True)
            exponentials = jnp.exp(scores - row_max)
            weights = (exponentials / jnp.sum(exponentials, axis=-1, keepdims=True)).astype(BF16)
            result = dot(weights, value).astype(BF16)
            rows_out = bucket // outputs
            for k, out in enumerate(outs):
                out[:, h, c] = result[k * rows_out : (k + 1) * rows_out].reshape(rows_out // slot, slot, HEAD_DIM)

            key = key.astype(F32)
            scaled = key * lax.rsqrt(jnp.mean(key * key, axis=-1, keepdims=True) + 1e-06)
            unit = (scaled / math.sqrt(HEAD_DIM)).astype(BF16).astype(F32)
            unit = jnp.where(key < FULL_BELOW, unit, 0.0)
            sums[c, h : h + 1] = jnp.sum(unit, axis=0, keepdims=True)


def attend(turn, received, streamed, outputs):
    spans, within, heads, clusters, slot, _ = received.shape
    together = 2
    per_output = spans * within // outputs
    block = pl.BlockSpec((spans, within, heads, together, slot, 3 * HEAD_DIM), lambda c, t: (0, 0, 0, c, 0, 0))
    return pl.pallas_call(
        functools.partial(attend_kernel, outputs, streamed),
        out_shape=[jax.ShapeDtypeStruct((per_output, heads, clusters, slot, HEAD_DIM), BF16)] * outputs
        + [jax.ShapeDtypeStruct((clusters, heads, HEAD_DIM), F32)],
        grid_spec=pltpu.PrefetchScalarGridSpec(
            num_scalar_prefetch=1,
            grid=(clusters // together,),
            in_specs=[block if streamed else VMEM_WHOLE],
            out_specs=[pl.BlockSpec((per_output, heads, together, slot, HEAD_DIM), lambda c, t: (0, 0, c, 0, 0))] * outputs
            + [pl.BlockSpec((together, heads, HEAD_DIM), lambda c, t: (c, 0, 0))],
        ),
        compiler_params=params(),
        name="attend",
    )(turn, received if streamed else in_vmem(received))


def regroup_kernel(turn, *refs):
    count = len(TURNS)
    pieces, outs, sems = refs[:-count - 1], refs[-count - 1 : -1], refs[-1]
    copies = []
    for k, (dz, dc) in enumerate(TURNS):
        at = ((turn[1] + dz) & 3) * 2 + (turn[2] ^ dc)
        for d, piece in enumerate(pieces):
            copies.append(pltpu.make_async_copy(piece.at[at], outs[k].at[d], sems.at[k, d]))
    for copy in copies:
        copy.start()
    for copy in copies:
        copy.wait()


def regroup(turn, pieces):
    shape = (len(pieces), *pieces[0].shape[1:])
    return pl.pallas_call(
        regroup_kernel,
        out_shape=[jax.ShapeDtypeStruct(shape, BF16)] * len(TURNS),
        grid_spec=pltpu.PrefetchScalarGridSpec(
            num_scalar_prefetch=1,
            grid=(1,),
            in_specs=[pl.BlockSpec(memory_space=pl.ANY)] * len(pieces),
            out_specs=[pl.BlockSpec(memory_space=pl.ANY)] * len(TURNS),
            scratch_shapes=[pltpu.SemaphoreType.DMA((len(TURNS), len(pieces)))],
        ),
        compiler_params=params(),
        name="regroup",
    )(turn, *pieces)


def unpack_kernel(count, *refs):
    pieces, slot_of, top, bottom = refs[:count], refs[count], refs[count + 1], refs[count + 2]
    half, width = top.shape
    source = [piece[:, pl.program_id(0)].reshape(-1, width) for piece in pieces]
    source = jnp.concatenate(source, axis=0) if count > 1 else source[0]
    slots = source.shape[0]
    chunk = 256
    iota = lax.broadcasted_iota(jnp.int32, (chunk, slots), 1)
    for start in range(0, 2 * half, chunk):
        onehot = jnp.where(iota == slot_of[0, start : start + chunk], 1.0, 0.0).astype(BF16)
        out, to = (top, start) if start < half else (bottom, start - half)
        out[to : to + chunk] = dot(onehot, source).astype(BF16)


def unpack(pieces, slot_cols):
    _, heads, _, _, width = pieces[0].shape
    rows = slot_cols.shape[1]
    return pl.pallas_call(
        functools.partial(unpack_kernel, len(pieces)),
        out_shape=(jax.ShapeDtypeStruct((rows // 2, heads * width), BF16),) * 2,
        grid=(heads,),
        in_specs=[VMEM_WHOLE] * len(pieces) + [pl.BlockSpec((1, rows, 1), lambda h: (h, 0, 0))],
        out_specs=(pl.BlockSpec((rows // 2, width), lambda h: (0, h)),) * 2,
        compiler_params=params(),
        name="unpack",
    )(*[in_vmem(piece) for piece in pieces], slot_cols)


def products_kernel(count, carried, *refs):
    pairs, weights = refs[carried : carried + 2 * count], refs[carried + 2 * count : carried + 3 * count]
    out = refs[-1]

    def add(side):
        total = refs[0][...] if carried else 0.0
        for k in range(count):
            total += dot(pairs[2 * k + side][...], weights[k][...])
        out[...] = total.astype(out.dtype)

    pl.when(pl.program_id(0) == 0)(lambda: add(0))
    pl.when(pl.program_id(0) == 1)(lambda: add(1))


def products(total, parts, chunk, kind):
    half, depth = parts[0][0].shape
    width = parts[0][2].shape[1]
    block = pl.BlockSpec((half, width), lambda i: (i, 0))
    carried = [] if total is None else [total]
    return pl.pallas_call(
        functools.partial(products_kernel, len(parts), len(carried)),
        out_shape=jax.ShapeDtypeStruct((2 * half, width), kind),
        grid=(2,),
        in_specs=[block] * len(carried)
        + [VMEM_WHOLE] * (2 * len(parts))
        + [pl.BlockSpec((depth, width), lambda i: (chunk, 0))] * len(parts),
        out_specs=block,
        compiler_params=params(),
        name="products",
    )(*carried, *[in_vmem(side) for part in parts for side in part[:2]], *[part[2] for part in parts])


def local(tokens, project_weights, output_weights, cluster_ids):
    seq_count = lax.axis_size(SEQ)
    groups = lax.axis_size("head")
    here = lax.axis_index("head")
    width = output_weights.shape[0]
    heads = width // HEAD_DIM
    rows = tokens.shape[0]
    half = rows // 2
    clusters = CLUST_DEV * seq_count

    assigned = cluster_ids[:, :, 0]
    matches = assigned[:, :, None] == jnp.arange(clusters, dtype=jnp.int32)
    row_iota = jnp.arange(rows, dtype=jnp.int32)
    earlier = (row_iota[None, :] < row_iota[:, None]).astype(BF16)
    before = jnp.einsum("ts,hsc->htc", earlier, matches.astype(BF16), preferred_element_type=F32)
    slot_rank = jnp.sum(jnp.where(matches, before, 0.0), axis=2).astype(jnp.int32)
    slot_index = assigned * SLOT + slot_rank
    slot_rows = slot_index[:, None, :]
    turn = jnp.stack([lax.axis_index(axis) for axis in SEQ]).astype(jnp.int32)

    weights = project_weights.transpose(1, 0, 2)
    where = jnp.stack([here, (here - 1) % groups, (here + 1) % groups, (here + 2) % groups]).astype(jnp.int32)

    top, bottom = tokens[:half], tokens[half:]
    left_top, right_bottom = shifted(top, 1), shifted(bottom, -1)
    left_bottom, right_top = shifted(bottom, 1), shifted(top, -1)
    left_top, right_bottom, slot_rows, where = lax.optimization_barrier((left_top, right_bottom, slot_rows, where))
    far_top, far_bottom = shifted(left_top, 1), shifted(right_bottom, -1)
    part = first_blocks(where, tokens, (left_top, left_bottom, right_top, right_bottom), weights)

    out_weights, far_top, far_bottom = lax.optimization_barrier((output_weights, far_top, far_bottom))
    out_blocks = []
    for by in range(groups):
        block = lax.dynamic_slice(out_weights, (0, (here + by) % groups * width), (width, width))
        out_blocks.append(shifted(block, by) if by else block)

    chunks = 2
    some = heads // chunks
    received = []
    for chunk in range(chunks):
        packed = pack(where, part, far_top, far_bottom, weights, slot_rows, seq_count, chunk, some)
        received.append(lax.all_to_all(packed, SEQ, 0, 0, tiled=True))

    def offset(by, count):
        return [(i, (i + by) % count) for i in range(count)]

    owned, gathered = [], []
    for chunk in range(chunks):
        early = chunk == 0
        slot_of = slot_index[chunk * some : (chunk + 1) * some]
        arrived = received[chunk].reshape(4, seq_count // 4, some, CLUST_DEV, SLOT, 3 * HEAD_DIM)
        *buckets, sums = attend(turn, arrived, early, 4 if early else 1)
        owned.append(sums)
        if early:
            pieces = list(buckets[:1]) + [lax.ppermute(buckets[d], SEQ[0], offset(d, 4)) for d in range(1, 4)]
            pieces = list(regroup(turn, pieces))
            for k, (dz, dc) in enumerate(TURNS):
                if k:
                    to = [(z * 2 + c, (z + dz) % 4 * 2 + (c ^ dc)) for z in range(4) for c in range(2)]
                    pieces[k] = lax.ppermute(pieces[k], SEQ[1:], to)
            owner = slot_of // (CLUST_DEV * SLOT)
            x, z, core = owner // 8, owner // 2 % 4, owner % 2
            piece = (((turn[1] - z) & 3) * 2 + (turn[2] ^ core)) * 4 + ((turn[0] - x) & 3)
            slot_of = piece * (CLUST_DEV * SLOT) + slot_of % (CLUST_DEV * SLOT)
        else:
            pieces = [lax.all_to_all(buckets[0], SEQ, 0, 0, tiled=True)]
        top, bottom = unpack(pieces, slot_of[:, :, None])
        left_top, right_bottom = shifted(top, 1), shifted(bottom, -1)
        left_bottom, right_top = shifted(bottom, 1), shifted(top, -1)
        far_top, far_bottom = shifted(left_top, 1), shifted(right_bottom, -1)
        gathered.append(((top, bottom), (left_top, left_bottom), (far_top, far_bottom), (right_top, right_bottom)))

    first, second = ([(*blocks[by], out_blocks[by]) for by in range(groups)] for blocks in gathered)
    total = products(None, first, 0, F32)
    total = products(total, second[:2] + second[3:], 1, F32)
    total = products(total, second[2:3], 1, BF16)
    owned = jnp.concatenate(owned, axis=1).transpose(1, 0, 2)
    return (total, owned)


def solution(mesh):
    split = Mesh(
        mesh.devices.reshape(4, 4, 2, mesh.shape["head"]), ("seq_0", "seq_1", "seq_2", "head")
    )
    in_specs = (P(SEQ, "head"), P(None, None, "head"), P("head", None), P("head", SEQ, None))
    out_specs = (P(SEQ, "head"), P("head", SEQ, None))
    return jax.shard_map(local, mesh=split, in_specs=in_specs, out_specs=out_specs, check_vma=False)
```

```python
import functools
import math

import jax
import jax.numpy as jnp
from jax import lax
from jax.experimental import pallas as pl
from jax.experimental.pallas import tpu as pltpu
from jax.sharding import Mesh
from jax.sharding import PartitionSpec as P


HEAD_DIM = 128
CLUST_DEV = 8
SLOT = 8
SEQ = ("seq_0", "seq_1", "seq_2")
F32 = jnp.float32
BF16 = jnp.bfloat16
EMPTY = float(1 << 20)
FULL_BELOW = float(1 << 19)


def shifted(array, by):
    count = lax.axis_size("head")
    return lax.ppermute(array, "head", [(i, (i + by) % count) for i in range(count)])


def in_vmem(array):
    return pltpu.with_memory_space_constraint(array, pltpu.VMEM)


VMEM_WHOLE = pl.BlockSpec(memory_space=pltpu.VMEM)


def params():
    return pltpu.CompilerParams(vmem_limit_bytes=56 * 1024 * 1024)


def dot(a, b):
    return jnp.dot(a, b, preferred_element_type=F32)


def early_blocks_kernel(where, own, left_top, right_bottom, w_own, w_left, w_right, out):
    half = left_top.shape[0]
    top, bottom = slice(0, half), slice(half, None)
    out[0, top] = dot(own[top], w_own[0]) + dot(left_top[...], w_left[0])
    out[0, bottom] = dot(own[bottom], w_own[0]) + dot(right_bottom[...], w_right[0])


def later_blocks_kernel(where, part, left_bottom, right_top, w_left, w_right, out):
    half = left_bottom.shape[0]
    top, bottom = slice(0, half), slice(half, None)
    out[0, top] = part[0, top] + dot(right_top[...], w_right[0])
    out[0, bottom] = part[0, bottom] + dot(left_bottom[...], w_left[0])


def weight_block(block, depth, width):
    return pl.BlockSpec((1, depth, width), lambda j, w: (j, w[block], 0))


def early_blocks(where, own, left_top, right_bottom, weights):
    kinds, _, width = weights.shape
    rows, depth = own.shape
    return pl.pallas_call(
        early_blocks_kernel,
        out_shape=jax.ShapeDtypeStruct((kinds, rows, width), F32),
        grid_spec=pltpu.PrefetchScalarGridSpec(
            num_scalar_prefetch=1,
            grid=(kinds,),
            in_specs=[pl.BlockSpec((rows, depth), lambda j, w: (0, 0)), VMEM_WHOLE, VMEM_WHOLE]
            + [weight_block(b, depth, width) for b in range(3)],
            out_specs=pl.BlockSpec((1, rows, width), lambda j, w: (j, 0, 0)),
        ),
        compiler_params=params(),
        name="early_blocks",
    )(where, own, in_vmem(left_top), in_vmem(right_bottom), weights, weights, weights)


def later_blocks(where, part, left_bottom, right_top, weights):
    kinds, rows, width = part.shape
    depth = left_bottom.shape[1]
    whole = pl.BlockSpec((1, rows, width), lambda j, w: (j, 0, 0))
    return pl.pallas_call(
        later_blocks_kernel,
        out_shape=jax.ShapeDtypeStruct((kinds, rows, width), F32),
        grid_spec=pltpu.PrefetchScalarGridSpec(
            num_scalar_prefetch=1,
            grid=(kinds,),
            in_specs=[whole, VMEM_WHOLE, VMEM_WHOLE] + [weight_block(b, depth, width) for b in (1, 2)],
            out_specs=whole,
        ),
        compiler_params=params(),
        name="later_blocks",
    )(where, part, in_vmem(left_bottom), in_vmem(right_top), weights, weights)


def pack_kernel(where, part, far_top, far_bottom, w_far, slot_of, out, projected):
    head = pl.program_id(0)
    kinds, rows, _ = part.shape
    half = rows // 2
    heads = projected.shape[0]

    @pl.when(head == 0)
    def _():
        for kind in range(kinds):
            to = slice(kind * HEAD_DIM, (kind + 1) * HEAD_DIM)
            for at, far in ((slice(0, half), far_top), (slice(half, rows), far_bottom)):
                done = (part[kind, at] + dot(far[...], w_far[kind])).astype(BF16)
                for h in range(heads):
                    projected[h, at, to] = done[:, h * HEAD_DIM : (h + 1) * HEAD_DIM]
        for h in range(heads):
            projected[h, :, kinds * HEAD_DIM :] = jnp.ones((rows, HEAD_DIM), BF16)

    rows_in = projected[head]
    slot_row = slot_of[0]
    devices, _, clusters, slot, _ = out.shape
    step = 4
    chunk = step * clusters * slot

    def body(i, carry):
        iota = lax.broadcasted_iota(jnp.int32, (chunk, rows), 0) + i * chunk
        onehot = jnp.where(iota == slot_row, 1.0, 0.0).astype(BF16)
        packed = dot(onehot, rows_in)
        at = pl.ds(i * step, step)
        for kind in range(kinds):
            block = packed[:, kind * HEAD_DIM : (kind + 1) * HEAD_DIM]
            if kind == 1:
                block = block + (EMPTY - EMPTY * packed[:, kinds * HEAD_DIM :])
            block = block.astype(BF16).reshape(step, clusters, slot, HEAD_DIM)
            out[at, 0, :, :, kind * HEAD_DIM : (kind + 1) * HEAD_DIM] = block
        return carry

    lax.fori_loop(0, devices // step, body, 0, unroll=2)


def pack(where, part, far_top, far_bottom, weights, slot_rows, devices, group, heads):
    kinds = weights.shape[0]
    rows = slot_rows.shape[2]
    width = heads * HEAD_DIM
    depth = far_top.shape[1]
    lanes = kinds * HEAD_DIM
    return pl.pallas_call(
        pack_kernel,
        out_shape=jax.ShapeDtypeStruct((devices, heads, CLUST_DEV, SLOT, lanes), BF16),
        grid_spec=pltpu.PrefetchScalarGridSpec(
            num_scalar_prefetch=1,
            grid=(heads,),
            in_specs=[
                pl.BlockSpec((kinds, rows, width), lambda h, w: (0, 0, group)),
                VMEM_WHOLE,
                VMEM_WHOLE,
                pl.BlockSpec((kinds, depth, width), lambda h, w: (0, w[3], group)),
                pl.BlockSpec((1, 1, rows), lambda h, w: (group * heads + h, 0, 0)),
            ],
            out_specs=pl.BlockSpec((devices, 1, CLUST_DEV, SLOT, lanes), lambda h, w: (0, h, 0, 0, 0)),
            scratch_shapes=[pltpu.VMEM((heads, rows, lanes + HEAD_DIM), BF16)],
        ),
        compiler_params=params(),
        name="pack",
    )(where, part, in_vmem(far_top), in_vmem(far_bottom), weights, slot_rows)


def attend_kernel(streamed, received, out, sums):
    devices, heads, _, slot, _ = received.shape
    bucket = devices * slot
    together = out.shape[2]
    scale = 1.0 / math.sqrt(HEAD_DIM)
    rows = lax.broadcasted_iota(jnp.int32, (bucket, bucket), 0)
    cols = lax.broadcasted_iota(jnp.int32, (bucket, bucket), 1)
    causal = cols <= rows
    first_lane = jnp.where(lax.broadcasted_iota(jnp.int32, (16, HEAD_DIM), 1) == 0, 1.0, 0.0).astype(BF16)
    for c in range(together):
        for h in range(heads):
            both = received[:, h, c if streamed else pl.program_id(0) * together + c].reshape(bucket, 3 * HEAD_DIM)
            query, key, value = (both[:, i * HEAD_DIM : (i + 1) * HEAD_DIM] for i in range(3))
            query = jnp.concatenate([query, first_lane], axis=0)
            product = lax.dot_general(query, key, (((1,), (1,)), ((), ())), preferred_element_type=F32)
            filled = product[bucket : bucket + 1] < FULL_BELOW
            scores = jnp.where(causal & filled, product[:bucket] * scale, -1e30)
            row_max = jnp.max(scores, axis=-1, keepdims=True)
            exponentials = jnp.exp(scores - row_max)
            weights = (exponentials / jnp.sum(exponentials, axis=-1, keepdims=True)).astype(BF16)
            out[:, h, c] = dot(weights, value).astype(BF16).reshape(devices, slot, HEAD_DIM)

            key = key.astype(F32)
            scaled = key * lax.rsqrt(jnp.mean(key * key, axis=-1, keepdims=True) + 1e-06)
            unit = (scaled / math.sqrt(HEAD_DIM)).astype(BF16).astype(F32)
            unit = jnp.where(key < FULL_BELOW, unit, 0.0)
            sums[c, h : h + 1] = jnp.sum(unit, axis=0, keepdims=True)


def attend(received, streamed):
    devices, heads, clusters, slot, _ = received.shape
    together = 2
    block = pl.BlockSpec((devices, heads, together, slot, 3 * HEAD_DIM), lambda c: (0, 0, c, 0, 0))
    return pl.pallas_call(
        functools.partial(attend_kernel, streamed),
        out_shape=(
            jax.ShapeDtypeStruct((devices, heads, clusters, slot, HEAD_DIM), BF16),
            jax.ShapeDtypeStruct((clusters, heads, HEAD_DIM), F32),
        ),
        grid=(clusters // together,),
        in_specs=[block if streamed else VMEM_WHOLE],
        out_specs=(
            pl.BlockSpec((devices, heads, together, slot, HEAD_DIM), lambda c: (0, 0, c, 0, 0)),
            pl.BlockSpec((together, heads, HEAD_DIM), lambda c: (c, 0, 0)),
        ),
        compiler_params=params(),
        name="attend",
    )(received if streamed else in_vmem(received))


def unpack_kernel(returned, slot_of, top, bottom):
    devices, _, clusters, slot, width = returned.shape
    slots = devices * clusters * slot
    half = top.shape[0]
    source = returned[:, pl.program_id(0)].reshape(slots, width)
    chunk = 256

    iota = lax.broadcasted_iota(jnp.int32, (chunk, slots), 1)
    for start in range(0, 2 * half, chunk):
        onehot = jnp.where(iota == slot_of[0, start : start + chunk], 1.0, 0.0).astype(BF16)
        out, to = (top, start) if start < half else (bottom, start - half)
        out[to : to + chunk] = dot(onehot, source).astype(BF16)


def unpack(returned, slot_cols, group):
    _, heads, _, _, width = returned.shape
    rows = slot_cols.shape[1]
    return pl.pallas_call(
        unpack_kernel,
        out_shape=(jax.ShapeDtypeStruct((rows // 2, heads * width), BF16),) * 2,
        grid=(heads,),
        in_specs=[VMEM_WHOLE, pl.BlockSpec((1, rows, 1), lambda h: (group * heads + h, 0, 0))],
        out_specs=(pl.BlockSpec((rows // 2, width), lambda h: (0, h)),) * 2,
        compiler_params=params(),
        name="unpack",
    )(in_vmem(returned), slot_cols)


def products_kernel(count, carried, *refs):
    pairs, weights = refs[carried : carried + 2 * count], refs[carried + 2 * count : carried + 3 * count]
    out = refs[-1]

    def add(side):
        total = refs[0][...] if carried else 0.0
        for k in range(count):
            total += dot(pairs[2 * k + side][...], weights[k][...])
        out[...] = total.astype(out.dtype)

    pl.when(pl.program_id(0) == 0)(lambda: add(0))
    pl.when(pl.program_id(0) == 1)(lambda: add(1))


def products(total, parts, chunk, kind, own):
    half, depth = parts[0][0].shape
    width = parts[0][2].shape[1]
    block = pl.BlockSpec((half, width), lambda i: (i, 0))
    fetched = pl.BlockSpec((half, depth), lambda i: (0, 0))
    carried = [] if total is None else [total]
    sides = [side for part in parts for side in part[:2]]
    here = 2 if own else 0
    return pl.pallas_call(
        functools.partial(products_kernel, len(parts), len(carried)),
        out_shape=jax.ShapeDtypeStruct((2 * half, width), kind),
        grid=(2,),
        in_specs=[block] * len(carried)
        + [fetched] * here
        + [VMEM_WHOLE] * (len(sides) - here)
        + [pl.BlockSpec((depth, width), lambda i: (chunk, 0))] * len(parts),
        out_specs=block,
        compiler_params=params(),
        name="products",
    )(*carried, *sides[:here], *[in_vmem(side) for side in sides[here:]], *[part[2] for part in parts])


def local(tokens, project_weights, output_weights, cluster_ids):
    seq_count = lax.axis_size(SEQ)
    groups = lax.axis_size("head")
    here = lax.axis_index("head")
    width = output_weights.shape[0]
    heads = width // HEAD_DIM
    rows = tokens.shape[0]
    half = rows // 2
    clusters = CLUST_DEV * seq_count

    assigned = cluster_ids[:, :, 0]
    matches = assigned[:, :, None] == jnp.arange(clusters, dtype=jnp.int32)
    row_iota = jnp.arange(rows, dtype=jnp.int32)
    earlier = (row_iota[None, :] < row_iota[:, None]).astype(BF16)
    before = jnp.einsum("ts,hsc->htc", earlier, matches.astype(BF16), preferred_element_type=F32)
    slot_rank = jnp.sum(jnp.where(matches, before, 0.0), axis=2).astype(jnp.int32)
    slot_index = assigned * SLOT + slot_rank
    slot_rows = slot_index[:, None, :]

    weights = project_weights.transpose(1, 0, 2)
    where = jnp.stack([here, (here - 1) % groups, (here + 1) % groups, (here + 2) % groups]).astype(jnp.int32)

    top, bottom = tokens[:half], tokens[half:]
    left_top, right_bottom = shifted(top, 1), shifted(bottom, -1)
    left_bottom, right_top = shifted(bottom, 1), shifted(top, -1)
    left_top, right_bottom, slot_rows, where = lax.optimization_barrier((left_top, right_bottom, slot_rows, where))
    far_top, far_bottom = shifted(left_top, 1), shifted(right_bottom, -1)
    part = early_blocks(where, tokens, left_top, right_bottom, weights)
    part = later_blocks(where, part, left_bottom, right_top, weights)

    out_weights, late_rows, far_top, far_bottom = lax.optimization_barrier(
        (output_weights, slot_rows, far_top, far_bottom)
    )
    slot_cols = late_rows[:, 0, :, None]
    out_blocks = []
    for by in range(groups):
        block = lax.dynamic_slice(out_weights, (0, (here + by) % groups * width), (width, width))
        out_blocks.append(shifted(block, by) if by else block)

    chunks = 2
    some = heads // chunks
    received = []
    for chunk in range(chunks):
        packed = pack(where, part, far_top, far_bottom, weights, slot_rows, seq_count, chunk, some)
        received.append(lax.all_to_all(packed, SEQ, 0, 0, tiled=True))

    owned, gathered = [], []
    for chunk in range(chunks):
        buckets, sums = attend(received[chunk], streamed=chunk == 0)
        owned.append(sums)
        returned = lax.all_to_all(buckets, SEQ, 0, 0, tiled=True)
        top, bottom = unpack(returned, slot_cols, chunk)
        left_top, right_bottom = shifted(top, 1), shifted(bottom, -1)
        left_bottom, right_top = shifted(bottom, 1), shifted(top, -1)
        far_top, far_bottom = shifted(left_top, 1), shifted(right_bottom, -1)
        gathered.append(((top, bottom), (left_top, left_bottom), (far_top, far_bottom), (right_top, right_bottom)))

    first, second = ([(*blocks[by], out_blocks[by]) for by in range(groups)] for blocks in gathered)
    total = products(None, first, 0, F32, own=True)
    total = products(total, second[:2] + second[3:], 1, F32, own=True)
    total = products(total, second[2:3], 1, BF16, own=False)
    owned = jnp.concatenate(owned, axis=1).transpose(1, 0, 2)
    return (total, owned)


def solution(mesh):
    split = Mesh(
        mesh.devices.reshape(4, 4, 2, mesh.shape["head"]), ("seq_0", "seq_1", "seq_2", "head")
    )
    in_specs = (P(SEQ, "head"), P(None, None, "head"), P("head", None), P("head", SEQ, None))
    out_specs = (P(SEQ, "head"), P("head", SEQ, None))
    return jax.shard_map(local, mesh=split, in_specs=in_specs, out_specs=out_specs, check_vma=False)
```

```python
import functools
import math

import jax
import jax.numpy as jnp
from jax import lax
from jax.experimental import pallas as pl
from jax.experimental.pallas import tpu as pltpu
from jax.sharding import Mesh
from jax.sharding import PartitionSpec as P


HEAD_DIM = 128
CLUST_DEV = 8
SLOT = 8
SEQ = ("seq_0", "seq_1", "seq_2")
F32 = jnp.float32
BF16 = jnp.bfloat16
EMPTY = float(1 << 20)
FULL_BELOW = float(1 << 19)


def shifted(array, by):
    count = lax.axis_size("head")
    return lax.ppermute(array, "head", [(i, (i + by) % count) for i in range(count)])


def in_vmem(array):
    return pltpu.with_memory_space_constraint(array, pltpu.VMEM)


VMEM_WHOLE = pl.BlockSpec(memory_space=pltpu.VMEM)


def params():
    return pltpu.CompilerParams(vmem_limit_bytes=56 * 1024 * 1024)


def dot(a, b):
    return jnp.dot(a, b, preferred_element_type=F32)


def halves_kernel(top_in, bottom_in, top, bottom):
    top[...] = top_in[...]
    bottom[...] = bottom_in[...]


def halves(array):
    rows, width = array.shape
    steps = 4
    block = (rows // 2 // steps, width)
    out = pl.BlockSpec(block, lambda i: (i, 0))
    return pl.pallas_call(
        halves_kernel,
        out_shape=(jax.ShapeDtypeStruct((rows // 2, width), array.dtype),) * 2,
        grid=(steps,),
        in_specs=[out, pl.BlockSpec(block, lambda i: (i + steps, 0))],
        out_specs=(out, out),
        compiler_params=params(),
        name="halves",
    )(array, array)


def columns_kernel(rows, out):
    count = rows.shape[2]
    out[0] = jnp.broadcast_to(rows[0], (8, count)).T[:, :1]


def columns(rows):
    heads, _, count = rows.shape
    return pl.pallas_call(
        columns_kernel,
        out_shape=jax.ShapeDtypeStruct((heads, count, 1), rows.dtype),
        grid=(heads,),
        in_specs=[pl.BlockSpec((1, 1, count), lambda h: (h, 0, 0))],
        out_specs=pl.BlockSpec((1, count, 1), lambda h: (h, 0, 0)),
        compiler_params=params(),
        name="columns",
    )(rows)


def first_blocks_kernel(where, own, left_top, left_bottom, right_top, right_bottom, w_own, w_left, w_right, out):
    half = left_top.shape[0]
    for part, left, right in ((slice(0, half), left_top, right_top), (slice(half, None), left_bottom, right_bottom)):
        total = dot(own[part], w_own[0])
        total += dot(left[...], w_left[0])
        total += dot(right[...], w_right[0])
        out[0, part] = total


def first_blocks(where, own, halves, weights):
    kinds, _, width = weights.shape
    rows, depth = own.shape
    return pl.pallas_call(
        first_blocks_kernel,
        out_shape=jax.ShapeDtypeStruct((kinds, rows, width), F32),
        grid_spec=pltpu.PrefetchScalarGridSpec(
            num_scalar_prefetch=1,
            grid=(kinds,),
            in_specs=[pl.BlockSpec((rows, depth), lambda j, w: (0, 0))]
            + [VMEM_WHOLE] * 4
            + [pl.BlockSpec((1, depth, width), functools.partial(lambda b, j, w: (j, w[b], 0), b)) for b in range(3)],
            out_specs=pl.BlockSpec((1, rows, width), lambda j, w: (j, 0, 0)),
        ),
        compiler_params=params(),
        name="first_blocks",
    )(where, own, *[in_vmem(half) for half in halves], weights, weights, weights)


def pack_kernel(where, part, far_top, far_bottom, w_far, slot_of, out, projected):
    head = pl.program_id(0)
    kinds, rows, _ = part.shape
    half = rows // 2
    heads = projected.shape[0]

    @pl.when(head == 0)
    def _():
        for kind in range(kinds):
            to = slice(kind * HEAD_DIM, (kind + 1) * HEAD_DIM)
            for at, far in ((slice(0, half), far_top), (slice(half, rows), far_bottom)):
                done = (part[kind, at] + dot(far[...], w_far[kind])).astype(BF16)
                for h in range(heads):
                    projected[h, at, to] = done[:, h * HEAD_DIM : (h + 1) * HEAD_DIM]
        for h in range(heads):
            projected[h, :, kinds * HEAD_DIM :] = jnp.ones((rows, HEAD_DIM), BF16)

    rows_in = projected[head]
    slot_row = slot_of[0]
    devices, _, clusters, slot, _ = out.shape
    step = 4
    chunk = step * clusters * slot

    def body(i, carry):
        iota = lax.broadcasted_iota(jnp.int32, (chunk, rows), 0) + i * chunk
        onehot = jnp.where(iota == slot_row, 1.0, 0.0).astype(BF16)
        packed = dot(onehot, rows_in)
        at = pl.ds(i * step, step)
        for kind in range(kinds):
            block = packed[:, kind * HEAD_DIM : (kind + 1) * HEAD_DIM]
            if kind == 1:
                block = block + (EMPTY - EMPTY * packed[:, kinds * HEAD_DIM :])
            block = block.astype(BF16).reshape(step, clusters, slot, HEAD_DIM)
            out[at, 0, :, :, kind * HEAD_DIM : (kind + 1) * HEAD_DIM] = block
        return carry

    lax.fori_loop(0, devices // step, body, 0, unroll=2)


def pack(where, part, far_top, far_bottom, weights, slot_rows, devices, group, heads):
    kinds = weights.shape[0]
    rows = slot_rows.shape[2]
    width = heads * HEAD_DIM
    depth = far_top.shape[1]
    lanes = kinds * HEAD_DIM
    return pl.pallas_call(
        pack_kernel,
        out_shape=jax.ShapeDtypeStruct((devices, heads, CLUST_DEV, SLOT, lanes), BF16),
        grid_spec=pltpu.PrefetchScalarGridSpec(
            num_scalar_prefetch=1,
            grid=(heads,),
            in_specs=[
                pl.BlockSpec((kinds, rows, width), lambda h, w: (0, 0, group)),
                VMEM_WHOLE,
                VMEM_WHOLE,
                pl.BlockSpec((kinds, depth, width), lambda h, w: (0, w[3], group)),
                pl.BlockSpec((1, 1, rows), lambda h, w: (group * heads + h, 0, 0)),
            ],
            out_specs=pl.BlockSpec((devices, 1, CLUST_DEV, SLOT, lanes), lambda h, w: (0, h, 0, 0, 0)),
            scratch_shapes=[pltpu.VMEM((heads, rows, lanes + HEAD_DIM), BF16)],
        ),
        compiler_params=params(),
        name="pack",
    )(where, part, in_vmem(far_top), in_vmem(far_bottom), weights, slot_rows)


def attend_kernel(streamed, received, out, sums):
    devices, heads, _, slot, _ = received.shape
    bucket = devices * slot
    together = out.shape[2]
    scale = 1.0 / math.sqrt(HEAD_DIM)
    rows = lax.broadcasted_iota(jnp.int32, (bucket, bucket), 0)
    cols = lax.broadcasted_iota(jnp.int32, (bucket, bucket), 1)
    causal = cols <= rows
    first_lane = jnp.where(lax.broadcasted_iota(jnp.int32, (16, HEAD_DIM), 1) == 0, 1.0, 0.0).astype(BF16)
    for c in range(together):
        for h in range(heads):
            both = received[:, h, c if streamed else pl.program_id(0) * together + c].reshape(bucket, 3 * HEAD_DIM)
            query, key, value = (both[:, i * HEAD_DIM : (i + 1) * HEAD_DIM] for i in range(3))
            query = jnp.concatenate([query, first_lane], axis=0)
            product = lax.dot_general(query, key, (((1,), (1,)), ((), ())), preferred_element_type=F32)
            filled = product[bucket : bucket + 1] < FULL_BELOW
            scores = jnp.where(causal & filled, product[:bucket] * scale, -1e30)
            row_max = jnp.max(scores, axis=-1, keepdims=True)
            exponentials = jnp.exp(scores - row_max)
            weights = (exponentials / jnp.sum(exponentials, axis=-1, keepdims=True)).astype(BF16)
            out[:, h, c] = dot(weights, value).astype(BF16).reshape(devices, slot, HEAD_DIM)

            key = key.astype(F32)
            scaled = key * lax.rsqrt(jnp.mean(key * key, axis=-1, keepdims=True) + 1e-06)
            unit = (scaled / math.sqrt(HEAD_DIM)).astype(BF16).astype(F32)
            unit = jnp.where(key < FULL_BELOW, unit, 0.0)
            sums[c, h : h + 1] = jnp.sum(unit, axis=0, keepdims=True)


def attend(received, streamed):
    devices, heads, clusters, slot, _ = received.shape
    together = 2
    block = pl.BlockSpec((devices, heads, together, slot, 3 * HEAD_DIM), lambda c: (0, 0, c, 0, 0))
    return pl.pallas_call(
        functools.partial(attend_kernel, streamed),
        out_shape=(
            jax.ShapeDtypeStruct((devices, heads, clusters, slot, HEAD_DIM), BF16),
            jax.ShapeDtypeStruct((clusters, heads, HEAD_DIM), F32),
        ),
        grid=(clusters // together,),
        in_specs=[block if streamed else VMEM_WHOLE],
        out_specs=(
            pl.BlockSpec((devices, heads, together, slot, HEAD_DIM), lambda c: (0, 0, c, 0, 0)),
            pl.BlockSpec((together, heads, HEAD_DIM), lambda c: (c, 0, 0)),
        ),
        compiler_params=params(),
        name="attend",
    )(received if streamed else in_vmem(received))


def unpack_kernel(returned, slot_of, top, bottom):
    devices, _, clusters, slot, width = returned.shape
    slots = devices * clusters * slot
    half = top.shape[0]
    source = returned[:, pl.program_id(0)].reshape(slots, width)
    chunk = 256

    iota = lax.broadcasted_iota(jnp.int32, (chunk, slots), 1)
    for start in range(0, 2 * half, chunk):
        onehot = jnp.where(iota == slot_of[0, start : start + chunk], 1.0, 0.0).astype(BF16)
        out, to = (top, start) if start < half else (bottom, start - half)
        out[to : to + chunk] = dot(onehot, source).astype(BF16)


def unpack(returned, slot_cols, group):
    _, heads, _, _, width = returned.shape
    rows = slot_cols.shape[1]
    return pl.pallas_call(
        unpack_kernel,
        out_shape=(jax.ShapeDtypeStruct((rows // 2, heads * width), BF16),) * 2,
        grid=(heads,),
        in_specs=[VMEM_WHOLE, pl.BlockSpec((1, rows, 1), lambda h: (group * heads + h, 0, 0))],
        out_specs=(pl.BlockSpec((rows // 2, width), lambda h: (0, h)),) * 2,
        compiler_params=params(),
        name="unpack",
    )(in_vmem(returned), slot_cols)


def products_kernel(count, carried, *refs):
    pairs, weights = refs[carried : carried + 2 * count], refs[carried + 2 * count : carried + 3 * count]
    out = refs[-1]
    rows = out.shape[0]
    per_side = pairs[0].shape[0] // rows
    step = pl.program_id(0)
    at = pl.ds(pl.multiple_of(step % per_side * rows, rows), rows)

    def add(side):
        total = refs[0][...] if carried else 0.0
        for k in range(count):
            total += dot(pairs[2 * k + side][at], weights[k][...])
        out[...] = total.astype(out.dtype)

    pl.when(step < per_side)(lambda: add(0))
    pl.when(step >= per_side)(lambda: add(1))


def products(total, parts, chunk, kind, own):
    half, depth = parts[0][0].shape
    width = parts[0][2].shape[1]
    steps = 4
    block = pl.BlockSpec((2 * half // steps, width), lambda i: (i, 0))
    fetched = pl.BlockSpec((half, depth), lambda i: (0, 0))
    carried = [] if total is None else [total]
    sides = [side for part in parts for side in part[:2]]
    here = 2 if own else 0
    return pl.pallas_call(
        functools.partial(products_kernel, len(parts), len(carried)),
        out_shape=jax.ShapeDtypeStruct((2 * half, width), kind),
        grid=(steps,),
        in_specs=[block] * len(carried)
        + [fetched] * here
        + [VMEM_WHOLE] * (len(sides) - here)
        + [pl.BlockSpec((depth, width), lambda i: (chunk, 0))] * len(parts),
        out_specs=block,
        compiler_params=params(),
        name="products",
    )(*carried, *sides[:here], *[in_vmem(side) for side in sides[here:]], *[part[2] for part in parts])


def local(tokens, project_weights, output_weights, cluster_ids):
    seq_count = lax.axis_size(SEQ)
    groups = lax.axis_size("head")
    here = lax.axis_index("head")
    width = output_weights.shape[0]
    heads = width // HEAD_DIM
    rows = tokens.shape[0]
    clusters = CLUST_DEV * seq_count

    assigned = cluster_ids[:, :, 0]
    matches = assigned[:, :, None] == jnp.arange(clusters, dtype=jnp.int32)
    row_iota = jnp.arange(rows, dtype=jnp.int32)
    earlier = (row_iota[None, :] < row_iota[:, None]).astype(BF16)
    before = jnp.einsum("ts,hsc->htc", earlier, matches.astype(BF16), preferred_element_type=F32)
    slot_rank = jnp.sum(jnp.where(matches, before, 0.0), axis=2).astype(jnp.int32)
    slot_index = assigned * SLOT + slot_rank
    slot_rows = slot_index[:, None, :]

    weights = project_weights.transpose(1, 0, 2)
    where = jnp.stack([here, (here - 1) % groups, (here + 1) % groups, (here + 2) % groups]).astype(jnp.int32)

    top, bottom = halves(tokens)
    left_top, right_bottom = shifted(top, 1), shifted(bottom, -1)
    left_bottom, right_top = shifted(bottom, 1), shifted(top, -1)
    left_top, right_bottom, slot_rows, where = lax.optimization_barrier((left_top, right_bottom, slot_rows, where))
    far_top, far_bottom = shifted(left_top, 1), shifted(right_bottom, -1)
    part = first_blocks(where, tokens, (left_top, left_bottom, right_top, right_bottom), weights)

    out_weights, late_rows, far_top, far_bottom = lax.optimization_barrier(
        (output_weights, slot_rows, far_top, far_bottom)
    )
    slot_cols = columns(late_rows)
    out_blocks = []
    for by in range(groups):
        block = lax.dynamic_slice(out_weights, (0, (here + by) % groups * width), (width, width))
        out_blocks.append(shifted(block, by) if by else block)

    chunks = 2
    some = heads // chunks
    received = []
    for chunk in range(chunks):
        packed = pack(where, part, far_top, far_bottom, weights, slot_rows, seq_count, chunk, some)
        received.append(lax.all_to_all(packed, SEQ, 0, 0, tiled=True))

    owned, gathered = [], []
    for chunk in range(chunks):
        buckets, sums = attend(received[chunk], streamed=chunk == 0)
        owned.append(sums)
        returned = lax.all_to_all(buckets, SEQ, 0, 0, tiled=True)
        top, bottom = unpack(returned, slot_cols, chunk)
        left_top, right_bottom = shifted(top, 1), shifted(bottom, -1)
        left_bottom, right_top = shifted(bottom, 1), shifted(top, -1)
        far_top, far_bottom = shifted(left_top, 1), shifted(right_bottom, -1)
        gathered.append(((top, bottom), (left_top, left_bottom), (far_top, far_bottom), (right_top, right_bottom)))

    first, second = ([(*blocks[by], out_blocks[by]) for by in range(groups)] for blocks in gathered)
    total = products(None, first, 0, F32, own=True)
    total = products(total, second[:2] + second[3:], 1, F32, own=True)
    total = products(total, second[2:3], 1, BF16, own=False)
    owned = jnp.concatenate(owned, axis=1).transpose(1, 0, 2)
    return (total, owned)


def solution(mesh):
    split = Mesh(
        mesh.devices.reshape(4, 4, 2, mesh.shape["head"]), ("seq_0", "seq_1", "seq_2", "head")
    )
    in_specs = (P(SEQ, "head"), P(None, None, "head"), P("head", None), P("head", SEQ, None))
    out_specs = (P(SEQ, "head"), P("head", SEQ, None))
    return jax.shard_map(local, mesh=split, in_specs=in_specs, out_specs=out_specs, check_vma=False)
```

```python
import functools
import math

import jax
import jax.numpy as jnp
from jax import lax
from jax.experimental import pallas as pl
from jax.experimental.pallas import tpu as pltpu
from jax.sharding import Mesh
from jax.sharding import PartitionSpec as P


HEAD_DIM = 128
CLUST_DEV = 8
SLOT = 8
SEQ = ("seq_0", "seq_1", "seq_2")
F32 = jnp.float32
BF16 = jnp.bfloat16
EMPTY = float(1 << 20)
FULL_BELOW = float(1 << 19)


def shifted(array, by):
    count = lax.axis_size("head")
    return lax.ppermute(array, "head", [(i, (i + by) % count) for i in range(count)])


def in_vmem(array):
    return pltpu.with_memory_space_constraint(array, pltpu.VMEM)


VMEM_WHOLE = pl.BlockSpec(memory_space=pltpu.VMEM)


def params():
    return pltpu.CompilerParams(vmem_limit_bytes=56 * 1024 * 1024)


def dot(a, b):
    return jnp.dot(a, b, preferred_element_type=F32)


def columns_kernel(rows, out):
    count = rows.shape[2]
    out[0] = jnp.broadcast_to(rows[0], (8, count)).T[:, :1]


def columns(rows):
    heads, _, count = rows.shape
    return pl.pallas_call(
        columns_kernel,
        out_shape=jax.ShapeDtypeStruct((heads, count, 1), rows.dtype),
        grid=(heads,),
        in_specs=[pl.BlockSpec((1, 1, count), lambda h: (h, 0, 0))],
        out_specs=pl.BlockSpec((1, count, 1), lambda h: (h, 0, 0)),
        compiler_params=params(),
        name="columns",
    )(rows)


def first_blocks_kernel(where, own, left_top, left_bottom, right_top, right_bottom, w_own, w_left, w_right, out):
    half = left_top.shape[0]
    for part, left, right in ((slice(0, half), left_top, right_top), (slice(half, None), left_bottom, right_bottom)):
        total = dot(own[part], w_own[0])
        total += dot(left[...], w_left[0])
        total += dot(right[...], w_right[0])
        out[0, part] = total


def first_blocks(where, own, halves, weights):
    kinds, _, width = weights.shape
    rows, depth = own.shape
    return pl.pallas_call(
        first_blocks_kernel,
        out_shape=jax.ShapeDtypeStruct((kinds, rows, width), F32),
        grid_spec=pltpu.PrefetchScalarGridSpec(
            num_scalar_prefetch=1,
            grid=(kinds,),
            in_specs=[pl.BlockSpec((rows, depth), lambda j, w: (0, 0))]
            + [VMEM_WHOLE] * 4
            + [pl.BlockSpec((1, depth, width), functools.partial(lambda b, j, w: (j, w[b], 0), b)) for b in range(3)],
            out_specs=pl.BlockSpec((1, rows, width), lambda j, w: (j, 0, 0)),
        ),
        compiler_params=params(),
        name="first_blocks",
    )(where, own, *[in_vmem(half) for half in halves], weights, weights, weights)


def pack_kernel(where, part, far_top, far_bottom, w_far, slot_of, out, projected):
    head = pl.program_id(0)
    kinds, rows, _ = part.shape
    half = rows // 2
    heads = projected.shape[0]

    @pl.when(head == 0)
    def _():
        for kind in range(kinds):
            to = slice(kind * HEAD_DIM, (kind + 1) * HEAD_DIM)
            for at, far in ((slice(0, half), far_top), (slice(half, rows), far_bottom)):
                done = (part[kind, at] + dot(far[...], w_far[kind])).astype(BF16)
                for h in range(heads):
                    projected[h, at, to] = done[:, h * HEAD_DIM : (h + 1) * HEAD_DIM]
        for h in range(heads):
            projected[h, :, kinds * HEAD_DIM :] = jnp.ones((rows, HEAD_DIM), BF16)

    rows_in = projected[head]
    slot_row = slot_of[0]
    devices, _, clusters, slot, _ = out.shape
    step = 16
    chunk = step * clusters * slot

    def body(i, carry):
        iota = lax.broadcasted_iota(jnp.int32, (chunk, rows), 0) + i * chunk
        onehot = jnp.where(iota == slot_row, 1.0, 0.0).astype(BF16)
        packed = dot(onehot, rows_in)
        at = pl.ds(i * step, step)
        for kind in range(kinds):
            block = packed[:, kind * HEAD_DIM : (kind + 1) * HEAD_DIM]
            if kind == 1:
                block = block + (EMPTY - EMPTY * packed[:, kinds * HEAD_DIM :])
            block = block.astype(BF16).reshape(step, clusters, slot, HEAD_DIM)
            out[at, 0, :, :, kind * HEAD_DIM : (kind + 1) * HEAD_DIM] = block
        return carry

    lax.fori_loop(0, devices // step, body, 0, unroll=2)


def pack(where, part, far_top, far_bottom, weights, slot_rows, devices, group, heads):
    kinds = weights.shape[0]
    rows = slot_rows.shape[2]
    width = heads * HEAD_DIM
    depth = far_top.shape[1]
    lanes = kinds * HEAD_DIM
    return pl.pallas_call(
        pack_kernel,
        out_shape=jax.ShapeDtypeStruct((devices, heads, CLUST_DEV, SLOT, lanes), BF16),
        grid_spec=pltpu.PrefetchScalarGridSpec(
            num_scalar_prefetch=1,
            grid=(heads,),
            in_specs=[
                pl.BlockSpec((kinds, rows, width), lambda h, w: (0, 0, group)),
                VMEM_WHOLE,
                VMEM_WHOLE,
                pl.BlockSpec((kinds, depth, width), lambda h, w: (0, w[3], group)),
                pl.BlockSpec((1, 1, rows), lambda h, w: (group * heads + h, 0, 0)),
            ],
            out_specs=pl.BlockSpec((devices, 1, CLUST_DEV, SLOT, lanes), lambda h, w: (0, h, 0, 0, 0)),
            scratch_shapes=[pltpu.VMEM((heads, rows, lanes + HEAD_DIM), BF16)],
        ),
        compiler_params=params(),
        name="pack",
    )(where, part, in_vmem(far_top), in_vmem(far_bottom), weights, slot_rows)


def attend_kernel(streamed, received, out, sums):
    devices, heads, _, slot, _ = received.shape
    bucket = devices * slot
    together = out.shape[2]
    scale = 1.0 / math.sqrt(HEAD_DIM)
    rows = lax.broadcasted_iota(jnp.int32, (bucket, bucket), 0)
    cols = lax.broadcasted_iota(jnp.int32, (bucket, bucket), 1)
    causal = cols <= rows
    first_lane = jnp.where(lax.broadcasted_iota(jnp.int32, (16, HEAD_DIM), 1) == 0, 1.0, 0.0).astype(BF16)
    for c in range(together):
        for h in range(heads):
            both = received[:, h, c if streamed else pl.program_id(0) * together + c].reshape(bucket, 3 * HEAD_DIM)
            query, key, value = (both[:, i * HEAD_DIM : (i + 1) * HEAD_DIM] for i in range(3))
            query = jnp.concatenate([query, first_lane], axis=0)
            product = lax.dot_general(query, key, (((1,), (1,)), ((), ())), preferred_element_type=F32)
            filled = product[bucket : bucket + 1] < FULL_BELOW
            scores = jnp.where(causal & filled, product[:bucket] * scale, -1e30)
            row_max = jnp.max(scores, axis=-1, keepdims=True)
            exponentials = jnp.exp(scores - row_max)
            weights = (exponentials / jnp.sum(exponentials, axis=-1, keepdims=True)).astype(BF16)
            out[:, h, c] = dot(weights, value).astype(BF16).reshape(devices, slot, HEAD_DIM)

            key = key.astype(F32)
            scaled = key * lax.rsqrt(jnp.mean(key * key, axis=-1, keepdims=True) + 1e-06)
            unit = (scaled / math.sqrt(HEAD_DIM)).astype(BF16).astype(F32)
            unit = jnp.where(key < FULL_BELOW, unit, 0.0)
            sums[c, h : h + 1] = jnp.sum(unit, axis=0, keepdims=True)


def attend(received, streamed):
    devices, heads, clusters, slot, _ = received.shape
    together = 2
    block = pl.BlockSpec((devices, heads, together, slot, 3 * HEAD_DIM), lambda c: (0, 0, c, 0, 0))
    return pl.pallas_call(
        functools.partial(attend_kernel, streamed),
        out_shape=(
            jax.ShapeDtypeStruct((devices, heads, clusters, slot, HEAD_DIM), BF16),
            jax.ShapeDtypeStruct((clusters, heads, HEAD_DIM), F32),
        ),
        grid=(clusters // together,),
        in_specs=[block if streamed else VMEM_WHOLE],
        out_specs=(
            pl.BlockSpec((devices, heads, together, slot, HEAD_DIM), lambda c: (0, 0, c, 0, 0)),
            pl.BlockSpec((together, heads, HEAD_DIM), lambda c: (c, 0, 0)),
        ),
        compiler_params=params(),
        name="attend",
    )(received if streamed else in_vmem(received))


def unpack_kernel(returned, slot_of, top, bottom):
    devices, _, clusters, slot, width = returned.shape
    slots = devices * clusters * slot
    half = top.shape[0]
    source = returned[:, pl.program_id(0)].reshape(slots, width)
    chunk = 256

    iota = lax.broadcasted_iota(jnp.int32, (chunk, slots), 1)
    for start in range(0, 2 * half, chunk):
        onehot = jnp.where(iota == slot_of[0, start : start + chunk], 1.0, 0.0).astype(BF16)
        out, to = (top, start) if start < half else (bottom, start - half)
        out[to : to + chunk] = dot(onehot, source).astype(BF16)


def unpack(returned, slot_cols, group):
    _, heads, _, _, width = returned.shape
    rows = slot_cols.shape[1]
    return pl.pallas_call(
        unpack_kernel,
        out_shape=(jax.ShapeDtypeStruct((rows // 2, heads * width), BF16),) * 2,
        grid=(heads,),
        in_specs=[VMEM_WHOLE, pl.BlockSpec((1, rows, 1), lambda h: (group * heads + h, 0, 0))],
        out_specs=(pl.BlockSpec((rows // 2, width), lambda h: (0, h)),) * 2,
        compiler_params=params(),
        name="unpack",
    )(in_vmem(returned), slot_cols)


def products_kernel(count, carried, *refs):
    pairs, weights = refs[carried : carried + 2 * count], refs[carried + 2 * count : carried + 3 * count]
    out = refs[-1]

    def add(side):
        total = refs[0][...] if carried else 0.0
        for k in range(count):
            total += dot(pairs[2 * k + side][...], weights[k][...])
        out[...] = total.astype(out.dtype)

    pl.when(pl.program_id(0) == 0)(lambda: add(0))
    pl.when(pl.program_id(0) == 1)(lambda: add(1))


def products(total, parts, chunk, kind, own):
    half, depth = parts[0][0].shape
    width = parts[0][2].shape[1]
    block = pl.BlockSpec((half, width), lambda i: (i, 0))
    fetched = pl.BlockSpec((half, depth), lambda i: (0, 0))
    carried = [] if total is None else [total]
    sides = [side for part in parts for side in part[:2]]
    here = 2 if own else 0
    return pl.pallas_call(
        functools.partial(products_kernel, len(parts), len(carried)),
        out_shape=jax.ShapeDtypeStruct((2 * half, width), kind),
        grid=(2,),
        in_specs=[block] * len(carried)
        + [fetched] * here
        + [VMEM_WHOLE] * (len(sides) - here)
        + [pl.BlockSpec((depth, width), lambda i: (chunk, 0))] * len(parts),
        out_specs=block,
        compiler_params=params(),
        name="products",
    )(*carried, *sides[:here], *[in_vmem(side) for side in sides[here:]], *[part[2] for part in parts])


def local(tokens, project_weights, output_weights, cluster_ids):
    seq_count = lax.axis_size(SEQ)
    groups = lax.axis_size("head")
    here = lax.axis_index("head")
    width = output_weights.shape[0]
    heads = width // HEAD_DIM
    rows = tokens.shape[0]
    clusters = CLUST_DEV * seq_count

    assigned = cluster_ids[:, :, 0]
    matches = assigned[:, :, None] == jnp.arange(clusters, dtype=jnp.int32)
    row_iota = jnp.arange(rows, dtype=jnp.int32)
    earlier = (row_iota[None, :] < row_iota[:, None]).astype(BF16)
    before = jnp.einsum("ts,hsc->htc", earlier, matches.astype(BF16), preferred_element_type=F32)
    slot_rank = jnp.sum(jnp.where(matches, before, 0.0), axis=2).astype(jnp.int32)
    slot_index = assigned * SLOT + slot_rank
    slot_rows = slot_index[:, None, :]

    weights = project_weights.transpose(1, 0, 2)
    where = jnp.stack([here, (here - 1) % groups, (here + 1) % groups, (here + 2) % groups]).astype(jnp.int32)

    half = rows // 2
    top, bottom = tokens[:half], tokens[half:]
    left_top, right_bottom = shifted(top, 1), shifted(bottom, -1)
    left_bottom, right_top = shifted(bottom, 1), shifted(top, -1)
    left_top, right_bottom, slot_rows, where = lax.optimization_barrier((left_top, right_bottom, slot_rows, where))
    far_top, far_bottom = shifted(left_top, 1), shifted(right_bottom, -1)
    part = first_blocks(where, tokens, (left_top, left_bottom, right_top, right_bottom), weights)

    out_weights, late_rows, far_top, far_bottom = lax.optimization_barrier(
        (output_weights, slot_rows, far_top, far_bottom)
    )
    slot_cols = columns(late_rows)
    out_blocks = []
    for by in range(groups):
        block = lax.dynamic_slice(out_weights, (0, (here + by) % groups * width), (width, width))
        out_blocks.append(shifted(block, by) if by else block)

    chunks = 2
    some = heads // chunks
    received = []
    for chunk in range(chunks):
        packed = pack(where, part, far_top, far_bottom, weights, slot_rows, seq_count, chunk, some)
        received.append(lax.all_to_all(packed, SEQ, 0, 0, tiled=True))

    owned, gathered = [], []
    for chunk in range(chunks):
        buckets, sums = attend(received[chunk], streamed=chunk == 0)
        owned.append(sums)
        returned = lax.all_to_all(buckets, SEQ, 0, 0, tiled=True)
        top, bottom = unpack(returned, slot_cols, chunk)
        left_top, right_bottom = shifted(top, 1), shifted(bottom, -1)
        left_bottom, right_top = shifted(bottom, 1), shifted(top, -1)
        far_top, far_bottom = shifted(left_top, 1), shifted(right_bottom, -1)
        gathered.append(((top, bottom), (left_top, left_bottom), (far_top, far_bottom), (right_top, right_bottom)))

    first, second = ([(*blocks[by], out_blocks[by]) for by in range(groups)] for blocks in gathered)
    total = products(None, first, 0, F32, own=True)
    total = products(total, second[:2] + second[3:], 1, F32, own=True)
    total = products(total, second[2:3], 1, BF16, own=False)
    owned = jnp.concatenate(owned, axis=1).transpose(1, 0, 2)
    return (total, owned)


def solution(mesh):
    split = Mesh(
        mesh.devices.reshape(4, 4, 2, mesh.shape["head"]), ("seq_0", "seq_1", "seq_2", "head")
    )
    in_specs = (P(SEQ, "head"), P(None, None, "head"), P("head", None), P("head", SEQ, None))
    out_specs = (P(SEQ, "head"), P("head", SEQ, None))
    return jax.shard_map(local, mesh=split, in_specs=in_specs, out_specs=out_specs, check_vma=False)
```

```python
import functools
import math

import jax
import jax.numpy as jnp
from jax import lax
from jax.experimental import pallas as pl
from jax.experimental.pallas import tpu as pltpu
from jax.sharding import Mesh
from jax.sharding import PartitionSpec as P


HEAD_DIM = 128
CLUST_DEV = 8
SLOT = 8
SEQ = ("seq_0", "seq_1", "seq_2")
F32 = jnp.float32
BF16 = jnp.bfloat16
EMPTY = float(1 << 20)
FULL_BELOW = float(1 << 19)


def shifted(array, by):
    count = lax.axis_size("head")
    return lax.ppermute(array, "head", [(i, (i + by) % count) for i in range(count)])


def in_vmem(array):
    return pltpu.with_memory_space_constraint(array, pltpu.VMEM)


VMEM_WHOLE = pl.BlockSpec(memory_space=pltpu.VMEM)


def params():
    return pltpu.CompilerParams(vmem_limit_bytes=56 * 1024 * 1024)


def dot(a, b):
    return jnp.dot(a, b, preferred_element_type=F32)


def first_blocks_kernel(where, own, left_top, left_bottom, right_top, right_bottom, w_own, w_left, w_right, out):
    half = left_top.shape[0]
    for part, left, right in ((slice(0, half), left_top, right_top), (slice(half, None), left_bottom, right_bottom)):
        total = dot(own[part], w_own[0])
        total += dot(left[...], w_left[0])
        total += dot(right[...], w_right[0])
        out[0, part] = total


def first_blocks(where, own, halves, weights):
    kinds, _, width = weights.shape
    rows, depth = own.shape
    return pl.pallas_call(
        first_blocks_kernel,
        out_shape=jax.ShapeDtypeStruct((kinds, rows, width), F32),
        grid_spec=pltpu.PrefetchScalarGridSpec(
            num_scalar_prefetch=1,
            grid=(kinds,),
            in_specs=[pl.BlockSpec((rows, depth), lambda j, w: (0, 0))]
            + [VMEM_WHOLE] * 4
            + [pl.BlockSpec((1, depth, width), functools.partial(lambda b, j, w: (j, w[b], 0), b)) for b in range(3)],
            out_specs=pl.BlockSpec((1, rows, width), lambda j, w: (j, 0, 0)),
        ),
        compiler_params=params(),
        name="first_blocks",
    )(where, own, *[in_vmem(half) for half in halves], weights, weights, weights)


def pack_kernel(where, part, far_top, far_bottom, w_far, slot_of, out, projected):
    head = pl.program_id(0)
    kinds, rows, _ = part.shape
    half = rows // 2
    heads = projected.shape[0]

    @pl.when(head == 0)
    def _():
        for kind in range(kinds):
            to = slice(kind * HEAD_DIM, (kind + 1) * HEAD_DIM)
            for at, far in ((slice(0, half), far_top), (slice(half, rows), far_bottom)):
                done = (part[kind, at] + dot(far[...], w_far[kind])).astype(BF16)
                for h in range(heads):
                    projected[h, at, to] = done[:, h * HEAD_DIM : (h + 1) * HEAD_DIM]
        for h in range(heads):
            projected[h, :, kinds * HEAD_DIM :] = jnp.ones((rows, HEAD_DIM), BF16)

    rows_in = projected[head]
    slot_row = slot_of[0]
    devices, _, clusters, slot, _ = out.shape
    step = 16
    chunk = step * clusters * slot

    def body(i, carry):
        iota = lax.broadcasted_iota(jnp.int32, (chunk, rows), 0) + i * chunk
        onehot = jnp.where(iota == slot_row, 1.0, 0.0).astype(BF16)
        packed = dot(onehot, rows_in)
        at = pl.ds(i * step, step)
        for kind in range(kinds):
            block = packed[:, kind * HEAD_DIM : (kind + 1) * HEAD_DIM]
            if kind == 1:
                block = block + (EMPTY - EMPTY * packed[:, kinds * HEAD_DIM :])
            block = block.astype(BF16).reshape(step, clusters, slot, HEAD_DIM)
            out[at, 0, :, :, kind * HEAD_DIM : (kind + 1) * HEAD_DIM] = block
        return carry

    lax.fori_loop(0, devices // step, body, 0, unroll=2)


def pack(where, part, far_top, far_bottom, weights, slot_rows, devices, group, heads):
    kinds = weights.shape[0]
    rows = slot_rows.shape[2]
    width = heads * HEAD_DIM
    depth = far_top.shape[1]
    lanes = kinds * HEAD_DIM
    return pl.pallas_call(
        pack_kernel,
        out_shape=jax.ShapeDtypeStruct((devices, heads, CLUST_DEV, SLOT, lanes), BF16),
        grid_spec=pltpu.PrefetchScalarGridSpec(
            num_scalar_prefetch=1,
            grid=(heads,),
            in_specs=[
                pl.BlockSpec((kinds, rows, width), lambda h, w: (0, 0, group)),
                VMEM_WHOLE,
                VMEM_WHOLE,
                pl.BlockSpec((kinds, depth, width), lambda h, w: (0, w[3], group)),
                pl.BlockSpec((1, 1, rows), lambda h, w: (group * heads + h, 0, 0)),
            ],
            out_specs=pl.BlockSpec((devices, 1, CLUST_DEV, SLOT, lanes), lambda h, w: (0, h, 0, 0, 0)),
            scratch_shapes=[pltpu.VMEM((heads, rows, lanes + HEAD_DIM), BF16)],
        ),
        compiler_params=params(),
        name="pack",
    )(where, part, in_vmem(far_top), in_vmem(far_bottom), weights, slot_rows)


def attend_kernel(streamed, received, out, sums):
    devices, heads, _, slot, _ = received.shape
    bucket = devices * slot
    together = out.shape[2]
    scale = 1.0 / math.sqrt(HEAD_DIM)
    rows = lax.broadcasted_iota(jnp.int32, (bucket, bucket), 0)
    cols = lax.broadcasted_iota(jnp.int32, (bucket, bucket), 1)
    causal = cols <= rows
    first_lane = jnp.where(lax.broadcasted_iota(jnp.int32, (16, HEAD_DIM), 1) == 0, 1.0, 0.0).astype(BF16)
    for c in range(together):
        for h in range(heads):
            both = received[:, h, c if streamed else pl.program_id(0) * together + c].reshape(bucket, 3 * HEAD_DIM)
            query, key, value = (both[:, i * HEAD_DIM : (i + 1) * HEAD_DIM] for i in range(3))
            query = jnp.concatenate([query, first_lane], axis=0)
            product = lax.dot_general(query, key, (((1,), (1,)), ((), ())), preferred_element_type=F32)
            filled = product[bucket : bucket + 1] < FULL_BELOW
            scores = jnp.where(causal & filled, product[:bucket] * scale, -1e30)
            row_max = jnp.max(scores, axis=-1, keepdims=True)
            exponentials = jnp.exp(scores - row_max)
            weights = (exponentials / jnp.sum(exponentials, axis=-1, keepdims=True)).astype(BF16)
            out[:, h, c] = dot(weights, value).astype(BF16).reshape(devices, slot, HEAD_DIM)

            key = key.astype(F32)
            scaled = key * lax.rsqrt(jnp.mean(key * key, axis=-1, keepdims=True) + 1e-06)
            unit = (scaled / math.sqrt(HEAD_DIM)).astype(BF16).astype(F32)
            unit = jnp.where(key < FULL_BELOW, unit, 0.0)
            sums[c, h : h + 1] = jnp.sum(unit, axis=0, keepdims=True)


def attend(received, streamed):
    devices, heads, clusters, slot, _ = received.shape
    together = 2
    block = pl.BlockSpec((devices, heads, together, slot, 3 * HEAD_DIM), lambda c: (0, 0, c, 0, 0))
    return pl.pallas_call(
        functools.partial(attend_kernel, streamed),
        out_shape=(
            jax.ShapeDtypeStruct((devices, heads, clusters, slot, HEAD_DIM), BF16),
            jax.ShapeDtypeStruct((clusters, heads, HEAD_DIM), F32),
        ),
        grid=(clusters // together,),
        in_specs=[block if streamed else VMEM_WHOLE],
        out_specs=(
            pl.BlockSpec((devices, heads, together, slot, HEAD_DIM), lambda c: (0, 0, c, 0, 0)),
            pl.BlockSpec((together, heads, HEAD_DIM), lambda c: (c, 0, 0)),
        ),
        compiler_params=params(),
        name="attend",
    )(received if streamed else in_vmem(received))


def unpack_kernel(returned, slot_of, top, bottom):
    half, width = top.shape
    source = returned[:, pl.program_id(0)].reshape(-1, width)
    slots = source.shape[0]
    iota = lax.broadcasted_iota(jnp.int32, (slots, half), 0)
    for k, out in enumerate((top, bottom)):
        onehot = jnp.where(iota == slot_of[0, :, k * half : (k + 1) * half], 1.0, 0.0).astype(BF16)
        rows = lax.dot_general(onehot, source, (((0,), (0,)), ((), ())), preferred_element_type=F32)
        out[...] = rows.astype(BF16)


def unpack(returned, slot_rows, group):
    _, heads, _, _, width = returned.shape
    rows = slot_rows.shape[2]
    return pl.pallas_call(
        unpack_kernel,
        out_shape=(jax.ShapeDtypeStruct((rows // 2, heads * width), BF16),) * 2,
        grid=(heads,),
        in_specs=[VMEM_WHOLE, pl.BlockSpec((1, 1, rows), lambda h: (group * heads + h, 0, 0))],
        out_specs=(pl.BlockSpec((rows // 2, width), lambda h: (0, h)),) * 2,
        compiler_params=params(),
        name="unpack",
    )(in_vmem(returned), slot_rows)


def products_kernel(count, carried, keep, kept, *refs):
    pairs, weights = refs[carried : carried + 2 * count], refs[carried + 2 * count : carried + 3 * count]
    out = refs[-1]
    rows = pairs[0].shape[0]

    def add(side):
        total = 0.0
        if carried:
            total = refs[0][pl.ds(pl.program_id(0) * rows, rows)] if kept else refs[0][...]
        for k in range(count):
            total += dot(pairs[2 * k + side][...], weights[k][...])
        out[pl.ds(side * rows, rows) if keep else slice(None)] = total.astype(out.dtype)

    pl.when(pl.program_id(0) == 0)(lambda: add(0))
    pl.when(pl.program_id(0) == 1)(lambda: add(1))


def products(total, parts, chunk, kind, own, keep=False, kept=False):
    half, depth = parts[0][0].shape
    width = parts[0][2].shape[1]
    block = pl.BlockSpec((half, width), lambda i: (i, 0))
    fetched = pl.BlockSpec((half, depth), lambda i: (0, 0))
    carried = [] if total is None else [in_vmem(total) if kept else total]
    sides = [side for part in parts for side in part[:2]]
    here = 2 if own else 0
    return pl.pallas_call(
        functools.partial(products_kernel, len(parts), len(carried), keep, kept),
        out_shape=(pltpu.VMEM if keep else jax.ShapeDtypeStruct)((2 * half, width), kind),
        grid=(2,),
        in_specs=[VMEM_WHOLE if kept else block] * len(carried)
        + [fetched] * here
        + [VMEM_WHOLE] * (len(sides) - here)
        + [pl.BlockSpec((depth, width), lambda i: (chunk, 0))] * len(parts),
        out_specs=VMEM_WHOLE if keep else block,
        compiler_params=params(),
        name="products",
    )(*carried, *sides[:here], *[in_vmem(side) for side in sides[here:]], *[part[2] for part in parts])


def local(tokens, project_weights, output_weights, cluster_ids):
    seq_count = lax.axis_size(SEQ)
    groups = lax.axis_size("head")
    here = lax.axis_index("head")
    width = output_weights.shape[0]
    heads = width // HEAD_DIM
    rows = tokens.shape[0]
    clusters = CLUST_DEV * seq_count

    assigned = cluster_ids[:, :, 0]
    matches = assigned[:, :, None] == jnp.arange(clusters, dtype=jnp.int32)
    row_iota = jnp.arange(rows, dtype=jnp.int32)
    earlier = (row_iota[None, :] < row_iota[:, None]).astype(BF16)
    before = jnp.einsum("ts,hsc->htc", earlier, matches.astype(BF16), preferred_element_type=F32)
    slot_rank = jnp.sum(jnp.where(matches, before, 0.0), axis=2).astype(jnp.int32)
    slot_index = assigned * SLOT + slot_rank
    slot_rows = slot_index[:, None, :]

    weights = project_weights.transpose(1, 0, 2)
    where = jnp.stack([here, (here - 1) % groups, (here + 1) % groups, (here + 2) % groups]).astype(jnp.int32)

    half = rows // 2
    top, bottom = tokens[:half], tokens[half:]
    left_top, right_bottom = shifted(top, 1), shifted(bottom, -1)
    left_bottom, right_top = shifted(bottom, 1), shifted(top, -1)
    left_top, right_bottom, slot_rows, where = lax.optimization_barrier((left_top, right_bottom, slot_rows, where))
    far_top, far_bottom = shifted(left_top, 1), shifted(right_bottom, -1)
    part = first_blocks(where, tokens, (left_top, left_bottom, right_top, right_bottom), weights)

    out_weights, far_top, far_bottom = lax.optimization_barrier((output_weights, far_top, far_bottom))
    out_blocks = []
    for by in range(groups):
        block = lax.dynamic_slice(out_weights, (0, (here + by) % groups * width), (width, width))
        out_blocks.append(shifted(block, by) if by else block)

    chunks = 2
    some = heads // chunks
    received = []
    for chunk in range(chunks):
        packed = pack(where, part, far_top, far_bottom, weights, slot_rows, seq_count, chunk, some)
        received.append(lax.all_to_all(packed, SEQ, 0, 0, tiled=True))

    owned, gathered = [], []
    for chunk in range(chunks):
        buckets, sums = attend(received[chunk], streamed=chunk == 0)
        owned.append(sums)
        returned = lax.all_to_all(buckets, SEQ, 0, 0, tiled=True)
        top, bottom = unpack(returned, slot_rows, chunk)
        left_top, right_bottom = shifted(top, 1), shifted(bottom, -1)
        left_bottom, right_top = shifted(bottom, 1), shifted(top, -1)
        far_top, far_bottom = shifted(left_top, 1), shifted(right_bottom, -1)
        gathered.append(((top, bottom), (left_top, left_bottom), (far_top, far_bottom), (right_top, right_bottom)))

    first, second = ([(*blocks[by], out_blocks[by]) for by in range(groups)] for blocks in gathered)
    total = products(None, first, 0, F32, own=True)
    total = products(total, second[:2] + second[3:], 1, F32, own=True, keep=True)
    total = products(total, second[2:3], 1, BF16, own=False, kept=True)
    owned = jnp.concatenate(owned, axis=1).transpose(1, 0, 2)
    return (total, owned)


def solution(mesh):
    split = Mesh(
        mesh.devices.reshape(4, 4, 2, mesh.shape["head"]), ("seq_0", "seq_1", "seq_2", "head")
    )
    in_specs = (P(SEQ, "head"), P(None, None, "head"), P("head", None), P("head", SEQ, None))
    out_specs = (P(SEQ, "head"), P("head", SEQ, None))
    return jax.shard_map(local, mesh=split, in_specs=in_specs, out_specs=out_specs, check_vma=False)
```

```python
import functools
import math

import jax
import jax.numpy as jnp
from jax import lax
from jax.experimental import pallas as pl
from jax.experimental.pallas import tpu as pltpu
from jax.sharding import Mesh
from jax.sharding import PartitionSpec as P


HEAD_DIM = 128
CLUST_DEV = 8
SLOT = 8
SEQ = ("seq_0", "seq_1", "seq_2")
F32 = jnp.float32
BF16 = jnp.bfloat16
EMPTY = float(1 << 20)
FULL_BELOW = float(1 << 19)


def shifted(array, by):
    count = lax.axis_size("head")
    return lax.ppermute(array, "head", [(i, (i + by) % count) for i in range(count)])


def in_vmem(array):
    return pltpu.with_memory_space_constraint(array, pltpu.VMEM)


VMEM_WHOLE = pl.BlockSpec(memory_space=pltpu.VMEM)


def params():
    return pltpu.CompilerParams(vmem_limit_bytes=56 * 1024 * 1024)


def dot(a, b):
    return jnp.dot(a, b, preferred_element_type=F32)


def first_blocks_kernel(where, own, left_top, left_bottom, right_top, right_bottom, w_own, w_left, w_right, out):
    half = left_top.shape[0]
    for part, left, right in ((slice(0, half), left_top, right_top), (slice(half, None), left_bottom, right_bottom)):
        total = dot(own[part], w_own[0])
        total += dot(left[...], w_left[0])
        total += dot(right[...], w_right[0])
        out[0, part] = total


def first_blocks(where, own, halves, weights):
    kinds, _, width = weights.shape
    rows, depth = own.shape
    return pl.pallas_call(
        first_blocks_kernel,
        out_shape=jax.ShapeDtypeStruct((kinds, rows, width), F32),
        grid_spec=pltpu.PrefetchScalarGridSpec(
            num_scalar_prefetch=1,
            grid=(kinds,),
            in_specs=[pl.BlockSpec((rows, depth), lambda j, w: (0, 0))]
            + [VMEM_WHOLE] * 4
            + [pl.BlockSpec((1, depth, width), functools.partial(lambda b, j, w: (j, w[b], 0), b)) for b in range(3)],
            out_specs=pl.BlockSpec((1, rows, width), lambda j, w: (j, 0, 0)),
        ),
        compiler_params=params(),
        name="first_blocks",
    )(where, own, *[in_vmem(half) for half in halves], weights, weights, weights)


def pack_kernel(where, part, far_top, far_bottom, w_far, slot_of, out, projected):
    head = pl.program_id(0)
    kinds, rows, _ = part.shape
    half = rows // 2
    heads = projected.shape[0]

    @pl.when(head == 0)
    def _():
        for kind in range(kinds):
            to = slice(kind * HEAD_DIM, (kind + 1) * HEAD_DIM)
            for at, far in ((slice(0, half), far_top), (slice(half, rows), far_bottom)):
                done = (part[kind, at] + dot(far[...], w_far[kind])).astype(BF16)
                for h in range(heads):
                    projected[h, at, to] = done[:, h * HEAD_DIM : (h + 1) * HEAD_DIM]
        for h in range(heads):
            projected[h, :, kinds * HEAD_DIM :] = jnp.ones((rows, HEAD_DIM), BF16)

    rows_in = projected[head]
    slot_row = slot_of[0]
    devices, _, clusters, slot, _ = out.shape
    step = 16
    chunk = step * clusters * slot

    def body(i, carry):
        iota = lax.broadcasted_iota(jnp.int32, (chunk, rows), 0) + i * chunk
        onehot = jnp.where(iota == slot_row, 1.0, 0.0).astype(BF16)
        packed = dot(onehot, rows_in)
        at = pl.ds(i * step, step)
        for kind in range(kinds):
            block = packed[:, kind * HEAD_DIM : (kind + 1) * HEAD_DIM]
            if kind == 1:
                block = block + (EMPTY - EMPTY * packed[:, kinds * HEAD_DIM :])
            block = block.astype(BF16).reshape(step, clusters, slot, HEAD_DIM)
            out[at, 0, :, :, kind * HEAD_DIM : (kind + 1) * HEAD_DIM] = block
        return carry

    lax.fori_loop(0, devices // step, body, 0, unroll=2)


def pack(where, part, far_top, far_bottom, weights, slot_rows, devices, group, heads):
    kinds = weights.shape[0]
    rows = slot_rows.shape[2]
    width = heads * HEAD_DIM
    depth = far_top.shape[1]
    lanes = kinds * HEAD_DIM
    return pl.pallas_call(
        pack_kernel,
        out_shape=jax.ShapeDtypeStruct((devices, heads, CLUST_DEV, SLOT, lanes), BF16),
        grid_spec=pltpu.PrefetchScalarGridSpec(
            num_scalar_prefetch=1,
            grid=(heads,),
            in_specs=[
                pl.BlockSpec((kinds, rows, width), lambda h, w: (0, 0, group)),
                VMEM_WHOLE,
                VMEM_WHOLE,
                pl.BlockSpec((kinds, depth, width), lambda h, w: (0, w[3], group)),
                pl.BlockSpec((1, 1, rows), lambda h, w: (group * heads + h, 0, 0)),
            ],
            out_specs=pl.BlockSpec((devices, 1, CLUST_DEV, SLOT, lanes), lambda h, w: (0, h, 0, 0, 0)),
            scratch_shapes=[pltpu.VMEM((heads, rows, lanes + HEAD_DIM), BF16)],
        ),
        compiler_params=params(),
        name="pack",
    )(where, part, in_vmem(far_top), in_vmem(far_bottom), weights, slot_rows)


def attend_kernel(streamed, received, out, sums):
    devices, heads, _, slot, _ = received.shape
    bucket = devices * slot
    together = out.shape[2]
    scale = 1.0 / math.sqrt(HEAD_DIM)
    rows = lax.broadcasted_iota(jnp.int32, (bucket, bucket), 0)
    cols = lax.broadcasted_iota(jnp.int32, (bucket, bucket), 1)
    causal = cols <= rows
    first_lane = jnp.where(lax.broadcasted_iota(jnp.int32, (16, HEAD_DIM), 1) == 0, 1.0, 0.0).astype(BF16)
    for c in range(together):
        for h in range(heads):
            both = received[:, h, c if streamed else pl.program_id(0) * together + c].reshape(bucket, 3 * HEAD_DIM)
            query, key, value = (both[:, i * HEAD_DIM : (i + 1) * HEAD_DIM] for i in range(3))
            query = jnp.concatenate([query, first_lane], axis=0)
            product = lax.dot_general(query, key, (((1,), (1,)), ((), ())), preferred_element_type=F32)
            filled = product[bucket : bucket + 1] < FULL_BELOW
            scores = jnp.where(causal & filled, product[:bucket] * scale, -1e30)
            row_max = jnp.max(scores, axis=-1, keepdims=True)
            exponentials = jnp.exp(scores - row_max)
            weights = (exponentials / jnp.sum(exponentials, axis=-1, keepdims=True)).astype(BF16)
            out[:, h, c] = dot(weights, value).astype(BF16).reshape(devices, slot, HEAD_DIM)

            key = key.astype(F32)
            scaled = key * lax.rsqrt(jnp.mean(key * key, axis=-1, keepdims=True) + 1e-06)
            unit = (scaled / math.sqrt(HEAD_DIM)).astype(BF16).astype(F32)
            unit = jnp.where(key < FULL_BELOW, unit, 0.0)
            sums[c, h : h + 1] = jnp.sum(unit, axis=0, keepdims=True)


def attend(received, streamed):
    devices, heads, clusters, slot, _ = received.shape
    together = 2
    block = pl.BlockSpec((devices, heads, together, slot, 3 * HEAD_DIM), lambda c: (0, 0, c, 0, 0))
    return pl.pallas_call(
        functools.partial(attend_kernel, streamed),
        out_shape=(
            jax.ShapeDtypeStruct((devices, heads, clusters, slot, HEAD_DIM), BF16),
            jax.ShapeDtypeStruct((clusters, heads, HEAD_DIM), F32),
        ),
        grid=(clusters // together,),
        in_specs=[block if streamed else VMEM_WHOLE],
        out_specs=(
            pl.BlockSpec((devices, heads, together, slot, HEAD_DIM), lambda c: (0, 0, c, 0, 0)),
            pl.BlockSpec((together, heads, HEAD_DIM), lambda c: (c, 0, 0)),
        ),
        compiler_params=params(),
        name="attend",
    )(received if streamed else in_vmem(received))


def unpack_kernel(returned, slot_of, top, bottom):
    half = top.shape[0]
    heads, width = returned.shape[1], returned.shape[-1]
    slots = returned.shape[0] * returned.shape[2] * returned.shape[3]
    iota = lax.broadcasted_iota(jnp.int32, (slots, half), 0)
    for head in range(heads):
        source = returned[:, head].reshape(slots, width)
        for k, out in enumerate((top, bottom)):
            onehot = jnp.where(iota == slot_of[head, :, k * half : (k + 1) * half], 1.0, 0.0).astype(BF16)
            rows = lax.dot_general(onehot, source, (((0,), (0,)), ((), ())), preferred_element_type=F32)
            out[:, head * width : (head + 1) * width] = rows.astype(BF16)


def unpack(returned, slot_rows, group):
    _, heads, _, _, width = returned.shape
    rows = slot_rows.shape[2]
    return pl.pallas_call(
        unpack_kernel,
        out_shape=(jax.ShapeDtypeStruct((rows // 2, heads * width), BF16),) * 2,
        grid=(1,),
        in_specs=[VMEM_WHOLE, pl.BlockSpec((heads, 1, rows), lambda i: (group, 0, 0))],
        out_specs=(pl.BlockSpec((rows // 2, heads * width), lambda i: (0, 0)),) * 2,
        compiler_params=params(),
        name="unpack",
    )(in_vmem(returned), slot_rows)


def products_kernel(count, carried, keep, kept, *refs):
    pairs, weights = refs[carried : carried + 2 * count], refs[carried + 2 * count : carried + 3 * count]
    out = refs[-1]
    rows = pairs[0].shape[0]

    def add(side):
        total = 0.0
        if carried:
            total = refs[0][pl.ds(pl.program_id(0) * rows, rows)] if kept else refs[0][...]
        for k in range(count):
            total += dot(pairs[2 * k + side][...], weights[k][...])
        out[pl.ds(side * rows, rows) if keep else slice(None)] = total.astype(out.dtype)

    pl.when(pl.program_id(0) == 0)(lambda: add(0))
    pl.when(pl.program_id(0) == 1)(lambda: add(1))


def products(total, parts, chunk, kind, own, keep=False, kept=False):
    half, depth = parts[0][0].shape
    width = parts[0][2].shape[1]
    block = pl.BlockSpec((half, width), lambda i: (i, 0))
    fetched = pl.BlockSpec((half, depth), lambda i: (0, 0))
    carried = [] if total is None else [in_vmem(total) if kept else total]
    sides = [side for part in parts for side in part[:2]]
    here = 2 if own else 0
    return pl.pallas_call(
        functools.partial(products_kernel, len(parts), len(carried), keep, kept),
        out_shape=(pltpu.VMEM if keep else jax.ShapeDtypeStruct)((2 * half, width), kind),
        grid=(2,),
        in_specs=[VMEM_WHOLE if kept else block] * len(carried)
        + [fetched] * here
        + [VMEM_WHOLE] * (len(sides) - here)
        + [pl.BlockSpec((depth, width), lambda i: (chunk, 0))] * len(parts),
        out_specs=VMEM_WHOLE if keep else block,
        compiler_params=params(),
        name="products",
    )(*carried, *sides[:here], *[in_vmem(side) for side in sides[here:]], *[part[2] for part in parts])


def local(tokens, project_weights, output_weights, cluster_ids):
    seq_count = lax.axis_size(SEQ)
    groups = lax.axis_size("head")
    here = lax.axis_index("head")
    width = output_weights.shape[0]
    heads = width // HEAD_DIM
    rows = tokens.shape[0]
    clusters = CLUST_DEV * seq_count

    assigned = cluster_ids[:, :, 0]
    matches = assigned[:, :, None] == jnp.arange(clusters, dtype=jnp.int32)
    row_iota = jnp.arange(rows, dtype=jnp.int32)
    earlier = (row_iota[None, :] < row_iota[:, None]).astype(BF16)
    before = jnp.einsum("ts,hsc->htc", earlier, matches.astype(BF16), preferred_element_type=F32)
    slot_rank = jnp.sum(jnp.where(matches, before, 0.0), axis=2).astype(jnp.int32)
    slot_index = assigned * SLOT + slot_rank
    slot_rows = slot_index[:, None, :]

    weights = project_weights.transpose(1, 0, 2)
    where = jnp.stack([here, (here - 1) % groups, (here + 1) % groups, (here + 2) % groups]).astype(jnp.int32)

    half = rows // 2
    top, bottom = tokens[:half], tokens[half:]
    left_top, right_bottom = shifted(top, 1), shifted(bottom, -1)
    left_bottom, right_top = shifted(bottom, 1), shifted(top, -1)
    left_top, right_bottom, slot_rows, where = lax.optimization_barrier((left_top, right_bottom, slot_rows, where))
    far_top, far_bottom = shifted(left_top, 1), shifted(right_bottom, -1)
    part = first_blocks(where, tokens, (left_top, left_bottom, right_top, right_bottom), weights)

    out_weights, far_top, far_bottom = lax.optimization_barrier((output_weights, far_top, far_bottom))
    out_blocks = []
    for by in range(groups):
        block = lax.dynamic_slice(out_weights, (0, (here + by) % groups * width), (width, width))
        out_blocks.append(shifted(block, by) if by else block)

    chunks = 2
    some = heads // chunks
    received = []
    for chunk in range(chunks):
        packed = pack(where, part, far_top, far_bottom, weights, slot_rows, seq_count, chunk, some)
        received.append(lax.all_to_all(packed, SEQ, 0, 0, tiled=True))

    owned, gathered = [], []
    for chunk in range(chunks):
        buckets, sums = attend(received[chunk], streamed=chunk == 0)
        owned.append(sums)
        returned = lax.all_to_all(buckets, SEQ, 0, 0, tiled=True)
        top, bottom = unpack(returned, slot_rows, chunk)
        left_top, right_bottom = shifted(top, 1), shifted(bottom, -1)
        left_bottom, right_top = shifted(bottom, 1), shifted(top, -1)
        far_top, far_bottom = shifted(left_top, 1), shifted(right_bottom, -1)
        gathered.append(((top, bottom), (left_top, left_bottom), (far_top, far_bottom), (right_top, right_bottom)))

    first, second = ([(*blocks[by], out_blocks[by]) for by in range(groups)] for blocks in gathered)
    total = products(None, first, 0, F32, own=True)
    total = products(total, second[:2] + second[3:], 1, F32, own=True, keep=True)
    total = products(total, second[2:3], 1, BF16, own=False, kept=True)
    owned = jnp.concatenate(owned, axis=1).transpose(1, 0, 2)
    return (total, owned)


def solution(mesh):
    split = Mesh(
        mesh.devices.reshape(4, 4, 2, mesh.shape["head"]), ("seq_0", "seq_1", "seq_2", "head")
    )
    in_specs = (P(SEQ, "head"), P(None, None, "head"), P("head", None), P("head", SEQ, None))
    out_specs = (P(SEQ, "head"), P("head", SEQ, None))
    return jax.shard_map(local, mesh=split, in_specs=in_specs, out_specs=out_specs, check_vma=False)
```
